256 devices in a mesh: pairs: 128 (over y, x, z), aux: 2 (over core).
Axes of the slice: x: 4, y: 4, z: 8, core: 2. Of those that a mesh axis runs over, the one named last changes fastest.
Arguments:
- blocks: bfloat16 [256, 2048, 256], P('pairs', 'aux'), may hold values from -0.9 to 0.9
- pair_orbs: int32 [2048, 2], P('pairs'), may hold values from 0 to 255, as said below
- pno_count: int32 [2048], P('pairs'), may hold values from 128 to 256
- amplitudes: bfloat16 [2048, 256, 256], P('pairs'), may hold values from -6 to 6
- margins: bfloat16 [2048, 4, 256, 256], P('pairs'), may hold values from -0.375 to 0.375
- couple_target: int32 [2048, 4], replicated, may hold values from 0 to 2047, as said below
- couple_weight: float32 [2048, 4], replicated, may hold values from -1 to 1
- pno_energy: float32 [2048, 256], P('pairs'), may hold values from 0.3 to 4
- occ_energy: float32 [256], replicated, may hold values from -2 to -0.3
Outputs:
- residual: float32 [2048, 256, 256], P('pairs', 'aux')
The draws below stay inside these ranges and needn't reach their ends.
Inputs may be any that keep to these rules, and one draw needn't show every extreme that they name: `pair_orbs`: the first orbital of pair p belongs to pairs index p // 16 (orbitals o with o // 2 equal to it); the second belongs to that index or an adjacent one. `couple_target`: every target of source pair q is held by pairs index q // 16 or an adjacent one (target t is held by index t // 16).
All inputs are finite; a program needn't handle non-finite values.
Results may differ from the reference program's by a relative error of at most 0.00076.
Values may be sent and summed in bfloat16 or wider, within the bound.
No kernel may reach another device: no remote copies, remote signals or barrier semaphores. Data moves between devices by JAX's collectives and lax.ppermute only.
A program may use at most 128 MiB of HBM per device.

```python
import math
import jax
import jax.numpy as jnp
from jax import lax

P_SIZE = 256
NAUX = 2048
PAIR_DEV = 16
ORB_DEV = 2
CPL = 4
HOLDERS = 128
NPAIR = 2048
NORB = 256


def scaled_field(key, shape, scale, bound):
    keys = jax.random.split(key, 1)
    values = jax.random.normal(keys[0], shape, jnp.float32) * scale
    return jnp.clip(values, -bound, bound)


def draw_blocks(key, part):
    return scaled_field(jax.random.fold_in(key, 51), (NORB, NAUX, P_SIZE), 0.15, 0.9).astype(jnp.bfloat16)


def draw_amplitudes(key, part):
    return scaled_field(jax.random.fold_in(key, 53), (NPAIR, P_SIZE, P_SIZE), 1.0, 6.0).astype(jnp.bfloat16)


def draw_margins(key, part):
    return scaled_field(jax.random.fold_in(key, 57), (NPAIR, CPL, P_SIZE, P_SIZE), 1.0 / P_SIZE ** 0.5, 0.375).astype(jnp.bfloat16)


def draw_pair_orbs(key, part):
    keys = jax.random.split(jax.random.fold_in(key, 11), 3)
    pair_ids = jnp.arange(NPAIR, dtype=jnp.int32)
    holder_ids = pair_ids // PAIR_DEV
    slot_ids = pair_ids % PAIR_DEV
    first_orb = holder_ids * ORB_DEV + jax.random.randint(keys[0], (NPAIR,), 0, ORB_DEV)
    steps_away = jax.random.randint(keys[1], (NPAIR,), -1, 2)
    steps_away = jnp.where(slot_ids == 0, -1, jnp.where(slot_ids == 1, 1, steps_away))
    other_holder = jnp.clip(holder_ids + steps_away, 0, HOLDERS - 1)
    second_orb = other_holder * ORB_DEV + jax.random.randint(keys[2], (NPAIR,), 0, ORB_DEV)
    first_orb = first_orb.at[0].set(0).at[NPAIR - 1].set(NORB - 1)
    second_orb = second_orb.at[0].set(0)
    return jnp.stack([first_orb, second_orb], axis=1).astype(jnp.int32)


def draw_pno_count(key, part):
    counts = jax.random.randint(jax.random.fold_in(key, 23), (NPAIR,), P_SIZE // 2, P_SIZE + 1)
    counts = counts.at[0].set(P_SIZE).at[1].set(P_SIZE // 2)
    return counts.astype(jnp.int32)


def draw_couple_target(key, part):
    keys = jax.random.split(jax.random.fold_in(key, 37), 2)
    pair_ids = jnp.arange(NPAIR, dtype=jnp.int32)[:, None]
    holder_ids = pair_ids // PAIR_DEV
    slot_ids = pair_ids % PAIR_DEV
    coupling_ids = jnp.arange(CPL, dtype=jnp.int32)[None, :]
    steps_away = jax.random.randint(keys[0], (NPAIR, CPL), -1, 2)
    steps_away = jnp.where((coupling_ids == 0) & (slot_ids == 0), -1, steps_away)
    steps_away = jnp.where((coupling_ids == 0) & (slot_ids == 1), 1, steps_away)
    target_holder = jnp.clip(holder_ids + steps_away, 0, HOLDERS - 1)
    targets = target_holder * PAIR_DEV + jax.random.randint(keys[1], (NPAIR, CPL), 0, PAIR_DEV)
    targets = targets.at[0, 1].set(0).at[NPAIR - 1, 1].set(NPAIR - 1)
    return targets.astype(jnp.int32)


def block_levels(key, dims, shards, least, top_value):
    factor_of = 1.0
    for position, parts in shards:
        draws = jax.random.uniform(jax.random.fold_in(jax.random.fold_in(key, 6), position), (parts,), jnp.float32, least / len(shards), top_value / len(shards))
        factor_of = factor_of * jnp.repeat(jnp.exp(draws), dims[position] // parts).reshape((-1,) + (1,) * (len(dims) - 1 - position))
    return factor_of


def setup_inputs(seed: int = 0) -> dict:
    splits = jax.random.split(jax.random.key(seed), 10)
    blocks = draw_blocks(jax.random.fold_in(splits[9], 71), 0)
    pair_orbs = draw_pair_orbs(jax.random.fold_in(splits[9], 71), 0)
    pno_count = draw_pno_count(jax.random.fold_in(splits[9], 71), 0)
    amplitudes = draw_amplitudes(jax.random.fold_in(splits[9], 71), 0)
    margins = draw_margins(jax.random.fold_in(splits[9], 71), 0)
    couple_target = draw_couple_target(jax.random.fold_in(splits[9], 71), 0)
    couple_weight = jnp.clip(jax.random.uniform(splits[6], (NPAIR, CPL), jnp.float32, -1.0, 1.0), -1.0, 1.0)
    pno_energy = jnp.clip(jnp.exp(math.log(4.0) - 2.5902671 * jax.random.uniform(splits[7], (NPAIR, P_SIZE), jnp.float32) ** block_levels(splits[7], (NPAIR, P_SIZE), ((0, 128),), -0.2, 0.2)), 0.3, 4.0)
    occ_energy = jnp.clip(jax.random.uniform(splits[8], (NORB,), jnp.float32, -2.0, -0.3), -2.0, -0.3)
    return dict(blocks=blocks, pair_orbs=pair_orbs, pno_count=pno_count, amplitudes=amplitudes, margins=margins, couple_target=couple_target, couple_weight=couple_weight, pno_energy=pno_energy, occ_energy=occ_energy)


def reference(blocks, pair_orbs, pno_count, amplitudes, margins, couple_target, couple_weight, pno_energy, occ_energy):
    positions = jnp.arange(P_SIZE, dtype=jnp.int32)

    def pair_base(pair_index):
        orb_first = pair_orbs[pair_index, 0]
        orb_second = pair_orbs[pair_index, 1]
        exchange_block = jnp.dot(blocks[orb_first].T, blocks[orb_second], preferred_element_type=jnp.float32)
        energies = pno_energy[pair_index]
        shift_value = occ_energy[orb_first] + occ_energy[orb_second]
        denominator = energies[:, None] + energies[None, :] - shift_value
        return exchange_block + denominator * amplitudes[pair_index].astype(jnp.float32)

    base_terms = lax.map(pair_base, jnp.arange(NPAIR, dtype=jnp.int32))

    def add_source(accumulated, source_index):
        for coupling_slot in range(CPL):
            margin = margins[source_index, coupling_slot]
            first_product = jnp.dot(margin, amplitudes[source_index], preferred_element_type=jnp.float32).astype(jnp.bfloat16)
            contribution = jnp.dot(first_product, margin.T, preferred_element_type=jnp.float32) * couple_weight[source_index, coupling_slot]
            accumulated = accumulated.at[couple_target[source_index, coupling_slot]].add(contribution)
        return accumulated, None

    coupling, unused = lax.scan(add_source, jnp.zeros((NPAIR, P_SIZE, P_SIZE), jnp.float32), jnp.arange(NPAIR, dtype=jnp.int32))
    pno_mask = (positions[None, :] < pno_count[:, None]).astype(jnp.float32)
    return (base_terms + coupling) * pno_mask[:, :, None] * pno_mask[:, None, :]
```

```python
import jax
import jax.numpy as jnp
from jax import lax
from jax.experimental import pallas as pl
from jax.experimental.pallas import tpu as pltpu
from jax.sharding import PartitionSpec as P

AXES = ("pairs", "aux")
BF16, F32 = jnp.bfloat16, jnp.float32
VMEM, SMEM = pltpu.VMEM, pltpu.SMEM
UNROLL = 4
MIB = 1 << 20


def toward(count, cross, flip):
    pairs = []
    for holder in range(count):
        for core in range(2):
            step = 1 if (core == 0) != flip else -1
            if 0 <= holder + step < count:
                dest = (1 - core) if cross else core
                pairs.append((2 * holder + core, 2 * (holder + step) + dest))
    return pairs


def nt_dot(a, b):
    return lax.dot_general(a, b, (((1,), (1,)), ((), ())), preferred_element_type=F32)


def tn_dot(a, b):
    return lax.dot_general(a, b, (((0,), (0,)), ((), ())), preferred_element_type=F32)


def coupling_kernel(core_ref, rel_ref, w_ref, amp_hbm, mar_hbm, msg_ref, own_ref,
                    mbuf, abuf, fbuf, dir_list, own_list, msem, asem):
    core = core_ref[0]
    sources, couplings = mar_hbm.shape[0], mar_hbm.shape[1]
    slots = msg_ref.shape[0]
    half = own_ref.shape[1]
    shift = 2 * slots * core - slots

    def mar_copy(k):
        return pltpu.make_async_copy(
            mar_hbm.at[k // couplings, k % couplings], mbuf.at[k], msem.at[k])

    def amp_copy(q):
        return pltpu.make_async_copy(amp_hbm.at[q], abuf.at[q], asem.at[q])

    def scan(q, carry):
        n_dir, n_own = carry
        amp_copy(q).start()
        for c in range(couplings):
            k = q * couplings + c
            r = rel_ref[c, q]
            d = r + shift
            is_dir = (d >= 0) & (d < slots)
            is_own = (r >= 0) & (r < slots)
            dir_list[n_dir] = k
            own_list[n_own] = k

            @pl.when(is_dir | is_own)
            def _():
                mar_copy(k).start()

            n_dir = n_dir + is_dir.astype(jnp.int32)
            n_own = n_own + is_own.astype(jnp.int32)
        return n_dir, n_own

    n_dir, n_own = lax.fori_loop(0, sources, scan, (jnp.int32(0), jnp.int32(0)))
    for u in range(UNROLL):
        dir_list[n_dir + u] = dir_list[0]
        own_list[n_own + u] = own_list[0]

    @pl.loop(0, slots)
    def _(s):
        msg_ref[s] = jnp.zeros(msg_ref.shape[1:], F32)
        own_ref[s] = jnp.zeros(own_ref.shape[1:], F32)

    def run(items, n, rows, row0, acc, offset, waited):
        def body(g, waited):
            ks = [items[g * UNROLL + u] for u in range(UNROLL)]
            last = ks[0] // couplings
            for u in range(UNROLL):
                @pl.when(g * UNROLL + u < n)
                def _(u=u):
                    mar_copy(ks[u]).wait()

                last = jnp.maximum(last, ks[u] // couplings)

            def wait_amp(q, x):
                amp_copy(q).wait()
                return x

            lax.fori_loop(waited, last + 1, wait_amp, 0)
            for u in range(UNROLL):
                left = mbuf[ks[u], pl.ds(row0, rows), :]
                fbuf[u, :rows] = jnp.dot(
                    left, abuf[ks[u] // couplings], preferred_element_type=F32).astype(BF16)
            for u in range(UNROLL):
                c, q = ks[u] % couplings, ks[u] // couplings
                live = g * UNROLL + u < n
                weight = jnp.where(live, w_ref[c, q], 0.0)
                slot = rel_ref[c, q] + offset
                acc[slot] += weight * nt_dot(fbuf[u, :rows], mbuf[ks[u]])
            return jnp.maximum(waited, last + 1)

        return lax.fori_loop(0, pl.cdiv(n, UNROLL), body, waited)

    waited = run(dir_list, n_dir, msg_ref.shape[1], 0, msg_ref, shift, jnp.int32(0))
    row0 = pl.multiple_of(core * half, half)
    waited = run(own_list, n_own, half, row0, own_ref, 0, waited)

    def drain(q, x):
        amp_copy(q).wait()
        return x

    lax.fori_loop(waited, sources, drain, 0)


def coupling(core, rel, weights, amplitudes, margins):
    pairs, width = amplitudes.shape[0], amplitudes.shape[1]
    couplings = margins.shape[1]
    total = pairs * couplings
    any_spec = pl.BlockSpec(memory_space=pltpu.HBM)
    smem_spec = pl.BlockSpec(memory_space=SMEM)
    vmem_spec = pl.BlockSpec(memory_space=VMEM)
    return pl.pallas_call(
        coupling_kernel,
        out_shape=(
            jax.ShapeDtypeStruct((pairs, width, width), F32),
            jax.ShapeDtypeStruct((pairs, width // 2, width), F32),
        ),
        in_specs=[smem_spec, smem_spec, smem_spec, any_spec, any_spec],
        out_specs=(vmem_spec, vmem_spec),
        scratch_shapes=[
            VMEM((total, width, width), BF16),
            VMEM((pairs, width, width), BF16),
            VMEM((UNROLL, width, width), BF16),
            SMEM((total + UNROLL,), jnp.int32),
            SMEM((total + UNROLL,), jnp.int32),
            pltpu.SemaphoreType.DMA((total,)),
            pltpu.SemaphoreType.DMA((pairs,)),
        ],
        compiler_params=pltpu.CompilerParams(vmem_limit_bytes=12 * MIB),
        cost_estimate=pl.CostEstimate(
            flops=4 * 64 * 128 * 256 * 256, bytes_accessed=16 * MIB, transcendentals=0),
        name="coupling",
    )(core, rel, weights, amplitudes, margins)


def message_kernel(half_ref, pick_ref, a_in, b_in, a_loc, b_loc, acc_ref, out_ref, prod):
    step = pl.program_id(0)
    per = out_ref.shape[0]

    @pl.when(step == 0)
    def _():
        for j in range(2):
            for i in range(2):
                prod[2 * j + i] = tn_dot(a_in[j], a_loc[i]) + tn_dot(b_in[j], b_loc[i])
        prod[4] = jnp.zeros(prod.shape[1:], F32)

    for s in range(per):
        pick = pick_ref[step * per + s]
        out_ref[s] = (acc_ref[s] + prod[pick]).astype(BF16)


def message(half, pick, a_in, b_in, a_loc, b_loc, acc, per=4):
    slots, width = acc.shape[0], acc.shape[2]
    rows = width // 2
    depth = a_in.shape[1]
    lhs = pl.BlockSpec((2, depth, rows), lambda s, half, pick: (0, 0, half[0]))
    rhs = pl.BlockSpec((2, depth, width), lambda s, half, pick: (0, 0, 0))
    return pl.pallas_call(
        message_kernel,
        grid_spec=pltpu.PrefetchScalarGridSpec(
            num_scalar_prefetch=2,
            grid=(slots // per,),
            in_specs=[lhs, lhs, rhs, rhs,
                      pl.BlockSpec((per, rows, width), lambda s, half, pick: (s, half[0], 0))],
            out_specs=pl.BlockSpec((per, rows, width), lambda s, half, pick: (s, 0, 0)),
            scratch_shapes=[VMEM((5, rows, width), F32)],
        ),
        out_shape=jax.ShapeDtypeStruct((slots, rows, width), BF16),
        compiler_params=pltpu.CompilerParams(vmem_limit_bytes=16 * MIB),
        cost_estimate=pl.CostEstimate(
            flops=8 * 2 * 128 * 256 * 512, bytes_accessed=5 * MIB, transcendentals=0),
        name="message",
    )(half, pick, a_in, b_in, a_loc, b_loc, acc)


def exchange_kernel(core_ref, a_in, b_in, a_loc, b_loc, blk, blk_all, out_ref):
    for i in range(2):
        for j in range(2):
            out_ref[0, 2 * i + j] = tn_dot(a_loc[i], a_in[j]) + tn_dot(b_loc[i], b_in[j])
            out_ref[0, 4 + 2 * i + j] = tn_dot(blk[i], blk_all[j])


def exchange(core, a_in, b_in, a_loc, b_loc, blocks):
    depth, width = a_in.shape[1], a_in.shape[2]
    rows = width // 2
    side = lambda g, core: (0, 0, g + core[0] - 2 * g * core[0])
    full = lambda g, core: (0, 0, 0)
    lhs = pl.BlockSpec((2, depth, rows), side)
    rhs = pl.BlockSpec((2, depth, width), full)
    return pl.pallas_call(
        exchange_kernel,
        grid_spec=pltpu.PrefetchScalarGridSpec(
            num_scalar_prefetch=1,
            grid=(2,),
            in_specs=[rhs, rhs, lhs, lhs,
                      pl.BlockSpec((2, blocks.shape[1], rows), side),
                      pl.BlockSpec((2, blocks.shape[1], width), full)],
            out_specs=pl.BlockSpec((1, 8, rows, width), lambda g, core: (g, 0, 0, 0)),
        ),
        out_shape=jax.ShapeDtypeStruct((2, 8, rows, width), F32),
        compiler_params=pltpu.CompilerParams(vmem_limit_bytes=12 * MIB),
        cost_estimate=pl.CostEstimate(
            flops=2 * 8 * 2 * 256 * 256 * 1024, bytes_accessed=6 * MIB, transcendentals=0),
        name="exchange",
    )(core, a_in, b_in, a_loc, b_loc, blocks, blocks)


def base_kernel(core_ref, keep_ix, recv_ix, fkeep, frecv, shift_ref, en_ref, amp_ref, own_ref,
                near_ref, keep_ref, recv_ref, out_ref):
    step = pl.program_id(0)
    per, rows, width = out_ref.shape
    core = core_ref[0]
    for s in range(per):
        p = step * per + s
        cols = en_ref[pl.ds(p, 1), :]
        side = jnp.where(core == 0, cols[:, :rows], cols[:, rows:])
        down = jnp.broadcast_to(side, (rows, rows)).T
        down = jnp.concatenate([down] * (width // rows), axis=1)
        denom = down + cols - shift_ref[p]
        value = denom * amp_ref[s].astype(F32) + own_ref[s] + near_ref[s].astype(F32)
        value += keep_ref[0, keep_ix[p]] * fkeep[p]
        value += recv_ref[recv_ix[p]] * frecv[p]
        out_ref[s] = value


def base(core, keep_ix, recv_ix, fkeep, frecv, shift, energy, amplitudes, own, near, both, recv, per=4):
    slots, rows, width = own.shape
    tile = pl.BlockSpec((per, rows, width), lambda s, core, *_: (s, 0, 0))
    return pl.pallas_call(
        base_kernel,
        grid_spec=pltpu.PrefetchScalarGridSpec(
            num_scalar_prefetch=6,
            grid=(slots // per,),
            in_specs=[
                pl.BlockSpec((slots, width), lambda s, core, *_: (0, 0)),
                pl.BlockSpec((per, rows, width), lambda s, core, *_: (s, core[0], 0)),
                tile, tile,
                pl.BlockSpec((1, 8, rows, width), lambda s, core, *_: (0, 0, 0, 0)),
                pl.BlockSpec((8, rows, width), lambda s, core, *_: (0, 0, 0)),
            ],
            out_specs=tile,
        ),
        out_shape=jax.ShapeDtypeStruct((slots, rows, width), F32),
        compiler_params=pltpu.CompilerParams(vmem_limit_bytes=16 * MIB),
        cost_estimate=pl.CostEstimate(
            flops=16 * 128 * 256 * 8, bytes_accessed=8 * MIB, transcendentals=0),
        name="base",
    )(core, keep_ix, recv_ix, fkeep, frecv, shift, energy, amplitudes, own, near, both, recv)


def final_kernel(core_ref, count_ref, base_ref, far_ref, out_ref):
    step = pl.program_id(0)
    per, rows, width = out_ref.shape
    row = lax.broadcasted_iota(jnp.int32, (rows, width), 0) + core_ref[0] * rows
    col = lax.broadcasted_iota(jnp.int32, (rows, width), 1)
    most = jnp.maximum(row, col)
    for s in range(per):
        value = base_ref[s] + far_ref[s].astype(F32)
        out_ref[s] = jnp.where(most < count_ref[step * per + s], value, 0.0)


def final(core, count, base_terms, far, per=4):
    slots, rows, width = base_terms.shape
    tile = pl.BlockSpec((per, rows, width), lambda s, *_: (s, 0, 0))
    return pl.pallas_call(
        final_kernel,
        grid_spec=pltpu.PrefetchScalarGridSpec(
            num_scalar_prefetch=2,
            grid=(slots // per,),
            in_specs=[tile, tile],
            out_specs=tile,
        ),
        out_shape=jax.ShapeDtypeStruct((slots, rows, width), F32),
        compiler_params=pltpu.CompilerParams(vmem_limit_bytes=8 * MIB),
        cost_estimate=pl.CostEstimate(
            flops=16 * 128 * 256 * 2, bytes_accessed=5 * MIB, transcendentals=0),
        name="final",
    )(core, count, base_terms, far)


def local(blocks, pair_orbs, pno_count, amplitudes, margins, couple_target, couple_weight,
          pno_energy, occ_energy):
    holder = lax.axis_index("pairs").astype(jnp.int32)
    core = lax.axis_index("aux").astype(jnp.int32)
    holders = lax.axis_size("pairs")
    pairs = amplitudes.shape[0]
    orbs = blocks.shape[0]
    depth = blocks.shape[1] // 2
    straight_in = toward(holders, False, True)
    cross_in = toward(holders, True, False)
    straight_out = toward(holders, False, False)
    swap = [(2 * h + c, 2 * h + 1 - c) for h in range(holders) for c in range(2)]

    a_loc = blocks[:, :depth]
    b_own = blocks[:, depth:]
    a_in = lax.ppermute(a_loc, AXES, straight_in)
    b_in = lax.ppermute(b_own, AXES, cross_in)
    b_loc = lax.ppermute(b_own, AXES, swap)
    near_orbs = lax.ppermute(pair_orbs, AXES, straight_in)

    core1 = core.reshape(1)
    rel = lax.dynamic_slice_in_dim(couple_target, holder * pairs, pairs, 0).T - holder * pairs
    weights = lax.dynamic_slice_in_dim(couple_weight, holder * pairs, pairs, 0).T
    msg_acc, own_acc = coupling(
        core1, rel, weights,
        pltpu.with_memory_space_constraint(amplitudes, pltpu.HBM),
        pltpu.with_memory_space_constraint(margins, pltpu.HBM))

    step = 1 - 2 * core
    first = jnp.clip(near_orbs[:, 0] - (holder + step) * orbs, 0, orbs - 1)
    second = near_orbs[:, 1] - holder * orbs
    mine = (second >= 0) & (second < orbs)
    pick = jnp.where(mine, orbs * first + second, 4)

    msg_near = message(core1, pick, a_in, b_in, a_loc, b_loc, msg_acc)
    near = lax.ppermute(msg_near, AXES, straight_out)
    msg_far = message(1 - core1, pick, a_in, b_in, a_loc, b_loc, msg_acc)
    far = lax.ppermute(msg_far, AXES, cross_in)
    both = exchange(core1, a_in, b_in, a_loc, b_loc, blocks)
    recv = lax.ppermute(both[1], AXES, swap)

    i_loc = pair_orbs[:, 0] - holder * orbs
    j_all = pair_orbs[:, 1]
    side = j_all // orbs - holder
    j_loc = j_all % orbs
    index = orbs * i_loc + j_loc
    index = jnp.where(side == 0, index + 4, index)
    fkeep = ((side == 0) | (side == step)).astype(F32)
    frecv = ((side == 0) | (side == -step)).astype(F32)
    orbital = jnp.arange(occ_energy.shape[0], dtype=jnp.int32)
    shift = jnp.sum(
        jnp.where(pair_orbs[:, 0:1] == orbital, occ_energy, 0.0)
        + jnp.where(pair_orbs[:, 1:2] == orbital, occ_energy, 0.0), axis=1)
    base_terms = base(core1, index, index, fkeep, frecv, shift, pno_energy, amplitudes, own_acc,
                      near, both, recv)
    return final(core1, pno_count, base_terms, far)


def solution(mesh):
    placed = (
        P("pairs", "aux", None),
        P("pairs", None),
        P("pairs"),
        P("pairs", None, None),
        P("pairs", None, None, None),
        P(),
        P(),
        P("pairs", None),
        P(),
    )
    return jax.shard_map(
        local, mesh=mesh, in_specs=placed, out_specs=P("pairs", "aux", None), check_vma=False
    )
```

```python
import jax
import jax.numpy as jnp
from jax import lax
from jax.experimental import pallas as pl
from jax.experimental.pallas import tpu as pltpu
from jax.sharding import PartitionSpec as P

AXES = ("pairs", "aux")
BF16, F32 = jnp.bfloat16, jnp.float32
VMEM, SMEM = pltpu.VMEM, pltpu.SMEM
UNROLL = 4
MIB = 1 << 20


def toward(count, cross, flip):
    pairs = []
    for holder in range(count):
        for core in range(2):
            step = 1 if (core == 0) != flip else -1
            if 0 <= holder + step < count:
                dest = (1 - core) if cross else core
                pairs.append((2 * holder + core, 2 * (holder + step) + dest))
    return pairs


def nt_dot(a, b):
    return lax.dot_general(a, b, (((1,), (1,)), ((), ())), preferred_element_type=F32)


def tn_dot(a, b):
    return lax.dot_general(a, b, (((0,), (0,)), ((), ())), preferred_element_type=F32)


def coupling_kernel(first_ref, rel_ref, w_ref, amp_hbm, mar_hbm, acc_ref,
                    mbuf, abuf, fbuf, items, msem, asem):
    sources, couplings = mar_hbm.shape[0], mar_hbm.shape[1]
    slots, rows = acc_ref.shape[0], acc_ref.shape[1]
    shift = first_ref[0]
    row0 = pl.multiple_of(first_ref[1], rows) if rows < mar_hbm.shape[2] else 0

    def mar_copy(k):
        return pltpu.make_async_copy(
            mar_hbm.at[k // couplings, k % couplings], mbuf.at[k], msem.at[k])

    def amp_copy(q):
        return pltpu.make_async_copy(amp_hbm.at[q], abuf.at[q], asem.at[q])

    def scan(q, n):
        amp_copy(q).start()
        for c in range(couplings):
            k = q * couplings + c
            slot = rel_ref[c, q] - shift
            mine = (slot >= 0) & (slot < slots)
            items[n] = k

            @pl.when(mine)
            def _():
                mar_copy(k).start()

            n = n + mine.astype(jnp.int32)
        return n

    n = lax.fori_loop(0, sources, scan, jnp.int32(0))
    for u in range(UNROLL):
        items[n + u] = items[0]

    @pl.loop(0, slots)
    def _(s):
        acc_ref[s] = jnp.zeros(acc_ref.shape[1:], F32)

    def wait_amp(q, x):
        amp_copy(q).wait()
        return x

    def body(g, waited):
        ks = [items[g * UNROLL + u] for u in range(UNROLL)]
        last = ks[0] // couplings
        for u in range(UNROLL):
            @pl.when(g * UNROLL + u < n)
            def _(u=u):
                mar_copy(ks[u]).wait()

            last = jnp.maximum(last, ks[u] // couplings)

        lax.fori_loop(waited, last + 1, wait_amp, 0)
        for u in range(UNROLL):
            left = mbuf[ks[u], pl.ds(row0, rows), :]
            fbuf[u] = jnp.dot(
                left, abuf[ks[u] // couplings], preferred_element_type=F32).astype(BF16)
        for u in range(UNROLL):
            c, q = ks[u] % couplings, ks[u] // couplings
            weight = jnp.where(g * UNROLL + u < n, w_ref[c, q], 0.0)
            acc_ref[rel_ref[c, q] - shift] += weight * nt_dot(fbuf[u], mbuf[ks[u]])
        return jnp.maximum(waited, last + 1)

    waited = lax.fori_loop(0, pl.cdiv(n, UNROLL), body, jnp.int32(0))
    lax.fori_loop(waited, sources, wait_amp, 0)


def coupling(first, rel, weights, amplitudes, margins, rows):
    pairs, width = amplitudes.shape[0], amplitudes.shape[1]
    total = pairs * margins.shape[1]
    any_spec = pl.BlockSpec(memory_space=pltpu.HBM)
    smem_spec = pl.BlockSpec(memory_space=SMEM)
    return pl.pallas_call(
        coupling_kernel,
        out_shape=jax.ShapeDtypeStruct((pairs, rows, width), F32),
        in_specs=[smem_spec, smem_spec, smem_spec, any_spec, any_spec],
        out_specs=pl.BlockSpec(memory_space=VMEM),
        scratch_shapes=[
            VMEM((total, width, width), BF16),
            VMEM((pairs, width, width), BF16),
            VMEM((UNROLL, rows, width), BF16),
            SMEM((total + UNROLL,), jnp.int32),
            pltpu.SemaphoreType.DMA((total,)),
            pltpu.SemaphoreType.DMA((pairs,)),
        ],
        compiler_params=pltpu.CompilerParams(vmem_limit_bytes=12 * MIB),
        cost_estimate=pl.CostEstimate(
            flops=2 * 22 * rows * 2 * 256 * 256, bytes_accessed=6 * MIB, transcendentals=0),
    )(first, rel, weights,
      pltpu.with_memory_space_constraint(amplitudes, pltpu.HBM),
      pltpu.with_memory_space_constraint(margins, pltpu.HBM))


def whole(kernel, out_shape, n_smem, n_vmem, limit, cost, **extra):
    vmem = pl.BlockSpec(memory_space=VMEM)
    return pl.pallas_call(
        kernel,
        out_shape=out_shape,
        in_specs=[pl.BlockSpec(memory_space=SMEM)] * n_smem + [vmem] * n_vmem,
        out_specs=jax.tree.map(lambda _: vmem, out_shape),
        compiler_params=pltpu.CompilerParams(vmem_limit_bytes=limit * MIB),
        cost_estimate=pl.CostEstimate(flops=cost[0], bytes_accessed=cost[1] * MIB, transcendentals=0),
        **extra,
    )


def message_kernel(half_ref, pick_ref, near_blk, blk, acc_ref, *rest):
    out_refs, prod = rest[:-1], rest[-1]
    rows = prod.shape[1]
    row0 = pl.multiple_of(half_ref[0] * rows, rows)
    for j in range(2):
        for i in range(2):
            prod[2 * j + i] = tn_dot(near_blk[j, :, pl.ds(row0, rows)], blk[i])
    prod[4] = jnp.zeros(prod.shape[1:], F32)
    start = 0
    for out in out_refs:
        @pl.loop(0, out.shape[0])
        def _(s, out=out, start=start):
            out[s] = (acc_ref[start + s, pl.ds(row0, rows), :]
                      + prod[pick_ref[start + s]]).astype(BF16)

        start += out.shape[0]


def message(half, pick, near_blk, blk, acc, chunks):
    width = acc.shape[2]
    rows = width // 2
    return whole(
        message_kernel,
        [jax.ShapeDtypeStruct((n, rows, width), BF16) for n in chunks],
        2, 3, 4, (4 * 2 * 128 * 256 * 1024, 4),
        scratch_shapes=[VMEM((5, rows, width), F32)],
    )(half, pick, near_blk, blk, acc)


def exchange_kernel(core_ref, near_blk, blk, keep_ref, send_ref):
    rows = keep_ref.shape[1]
    for out, side in ((keep_ref, core_ref[0]), (send_ref, 1 - core_ref[0])):
        row0 = pl.multiple_of(side * rows, rows)
        for i in range(2):
            left = blk[i, :, pl.ds(row0, rows)]
            for j in range(2):
                out[2 * i + j] = tn_dot(left, near_blk[j])
                out[4 + 2 * i + j] = tn_dot(left, blk[j])


def exchange(core, near_blk, blk):
    width = blk.shape[2]
    half = jax.ShapeDtypeStruct((8, width // 2, width), F32)
    return whole(
        exchange_kernel, [half, half], 1, 2, 4, (16 * 2 * 128 * 256 * 1024, 4),
    )(core, near_blk, blk)


def base_kernel(core_ref, ix_ref, fkeep, frecv, shift_ref, en_ref, amp_ref, own_ref,
                near_ref, keep_ref, recv_ref, out_ref):
    slots, rows, width = out_ref.shape
    core = core_ref[0]
    row0 = pl.multiple_of(core * rows, rows)

    @pl.loop(0, slots)
    def _(p):
        cols = en_ref[pl.ds(p, 1), :]
        side = jnp.where(core == 0, cols[:, :rows], cols[:, rows:])
        down = jnp.broadcast_to(side, (rows, rows)).T
        down = jnp.concatenate([down] * (width // rows), axis=1)
        denom = down + cols - shift_ref[p]
        value = denom * amp_ref[p, pl.ds(row0, rows), :].astype(F32)
        value += own_ref[p] + near_ref[p].astype(F32)
        value += keep_ref[ix_ref[p]] * fkeep[p]
        value += recv_ref[ix_ref[p]] * frecv[p]
        out_ref[p] = value


def base(core, index, fkeep, frecv, shift, energy, amplitudes, own, near, keep, recv):
    return whole(
        base_kernel, jax.ShapeDtypeStruct(own.shape, F32), 5, 6, 4, (16 * 128 * 256 * 8, 8),
    )(core, index, fkeep, frecv, shift, energy, amplitudes, own, near, keep, recv)


def final_kernel(start, core_ref, count_ref, base_ref, far_ref, *rest):
    out_hbm, buf, sem = rest[-3:]
    slots, rows, width = far_ref.shape
    row = lax.broadcasted_iota(jnp.int32, (rows, width), 0) + core_ref[0] * rows
    col = lax.broadcasted_iota(jnp.int32, (rows, width), 1)
    most = jnp.maximum(row, col)

    def put(s):
        return pltpu.make_async_copy(buf.at[s], out_hbm.at[start + s], sem.at[s])

    @pl.loop(0, slots)
    def _(s):
        value = base_ref[start + s] + far_ref[s].astype(F32)
        buf[s] = jnp.where(most < count_ref[start + s], value, 0.0)
        put(s).start()

    @pl.loop(0, slots)
    def _(s):
        put(s).wait()


def final(start, core, count, base_terms, far, earlier=None):
    slots, rows, width = far.shape
    smem = pl.BlockSpec(memory_space=SMEM)
    vmem = pl.BlockSpec(memory_space=VMEM)
    hbm = pl.BlockSpec(memory_space=pltpu.HBM)
    more = [] if earlier is None else [earlier]

    def kernel(*refs):
        final_kernel(start, *refs)

    return pl.pallas_call(
        kernel,
        out_shape=jax.ShapeDtypeStruct(base_terms.shape, F32),
        in_specs=[smem, smem, vmem, vmem] + [hbm] * len(more),
        out_specs=hbm,
        scratch_shapes=[VMEM((slots, rows, width), F32), pltpu.SemaphoreType.DMA((slots,))],
        input_output_aliases={4: 0} if more else {},
        compiler_params=pltpu.CompilerParams(vmem_limit_bytes=4 * MIB),
        cost_estimate=pl.CostEstimate(
            flops=slots * 128 * 256 * 2, bytes_accessed=slots * MIB // 4, transcendentals=0),
    )(core, count, base_terms, far, *more)


def local(blocks, pair_orbs, pno_count, amplitudes, margins, couple_target, couple_weight,
          pno_energy, occ_energy):
    holder = lax.axis_index("pairs").astype(jnp.int32)
    core = lax.axis_index("aux").astype(jnp.int32)
    holders = lax.axis_size("pairs")
    pairs, width = amplitudes.shape[0], amplitudes.shape[1]
    orbs = blocks.shape[0]
    straight_in = toward(holders, False, True)
    straight_out = toward(holders, False, False)
    cross_out = toward(holders, True, False)
    swap = [(2 * h + c, 2 * h + 1 - c) for h in range(holders) for c in range(2)]

    near_blk = lax.ppermute(blocks, AXES, straight_in)
    near_orbs = lax.ppermute(pair_orbs, AXES, straight_in)

    core1 = core.reshape(1)
    rel = lax.dynamic_slice_in_dim(couple_target, holder * pairs, pairs, 0).T - holder * pairs
    weights = lax.dynamic_slice_in_dim(couple_weight, holder * pairs, pairs, 0).T
    step = 1 - 2 * core
    toward_first = jnp.stack([step * pairs, jnp.int32(0)])
    msg_acc = coupling(toward_first, rel, weights, amplitudes, margins, width)

    first = jnp.clip(near_orbs[:, 0] - (holder + step) * orbs, 0, orbs - 1)
    second = near_orbs[:, 1] - holder * orbs
    pick = jnp.where((second >= 0) & (second < orbs), orbs * first + second, 4)
    chunks = [pairs * 3 // 4, pairs - pairs * 3 // 4]
    msg_near, = message(core1, pick, near_blk, blocks, msg_acc, [pairs])
    near = lax.ppermute(msg_near, AXES, straight_out)
    msg_far = message(1 - core1, pick, near_blk, blocks, msg_acc, chunks)
    far = lax.ppermute(msg_far[0], AXES, cross_out)
    last = lax.ppermute(msg_far[1], AXES, cross_out)

    keep, send = exchange(core1, near_blk, blocks)
    recv = lax.ppermute(send, AXES, swap)
    own_first = jnp.stack([jnp.int32(0), core * (width // 2)])
    own = coupling(own_first, rel, weights, amplitudes, margins, width // 2)

    j_all = pair_orbs[:, 1]
    side = j_all // orbs - holder
    index = orbs * (pair_orbs[:, 0] - holder * orbs) + j_all % orbs
    index = jnp.where(side == 0, index + 4, index)
    fkeep = ((side == 0) | (side == step)).astype(F32)
    frecv = ((side == 0) | (side == -step)).astype(F32)
    orbital = jnp.arange(occ_energy.shape[0], dtype=jnp.int32)
    shift = jnp.sum(
        jnp.where(pair_orbs[:, 0:1] == orbital, occ_energy, 0.0)
        + jnp.where(pair_orbs[:, 1:2] == orbital, occ_energy, 0.0), axis=1)
    base_terms = base(core1, index, fkeep, frecv, shift, pno_energy, amplitudes, own, near,
                      keep, recv)
    out = final(0, core1, pno_count, base_terms, far)
    return final(chunks[0], core1, pno_count, base_terms, last, out)


def solution(mesh):
    placed = (
        P("pairs", "aux", None),
        P("pairs", None),
        P("pairs"),
        P("pairs", None, None),
        P("pairs", None, None, None),
        P(),
        P(),
        P("pairs", None),
        P(),
    )

    return jax.shard_map(
        local, mesh=mesh, in_specs=placed, out_specs=P("pairs", "aux", None), check_vma=False
    )
```

```python
import functools

import jax
import jax.numpy as jnp
from jax import lax
from jax.experimental import pallas as pl
from jax.experimental.pallas import tpu as pltpu
from jax.sharding import PartitionSpec as P

AXES = ("pairs", "aux")
BF16, F32 = jnp.bfloat16, jnp.float32
VMEM, SMEM = pltpu.VMEM, pltpu.SMEM
UNROLL = 4
MIB = 1 << 20


def toward(count, cross, flip):
    pairs = []
    for holder in range(count):
        for core in range(2):
            step = 1 if (core == 0) != flip else -1
            if 0 <= holder + step < count:
                dest = (1 - core) if cross else core
                pairs.append((2 * holder + core, 2 * (holder + step) + dest))
    return pairs


def nt_dot(a, b):
    return lax.dot_general(a, b, (((1,), (1,)), ((), ())), preferred_element_type=F32)


def tn_dot(a, b):
    return lax.dot_general(a, b, (((0,), (0,)), ((), ())), preferred_element_type=F32)


def coupling_kernel(early, meta_ref, rel_ref, w_ref, amp_hbm, mar_hbm, acc_ref, *rest):
    (far_ref, early_ref), rest = (rest[:2], rest[2:]) if early else ((None, None), rest)
    mbuf, fbuf, items, msem = rest[:4]
    abuf, asem = rest[4:] if early else (amp_hbm, None)
    sources, couplings = mar_hbm.shape[0], mar_hbm.shape[1]
    slots, rows = acc_ref.shape[0], acc_ref.shape[1]
    core = meta_ref[1]
    shift = (1 - 2 * core) * slots if early else 0
    row0 = pl.multiple_of(core * rows, rows)
    far0 = pl.multiple_of(rows - core * rows, rows)

    def mar_copy(k):
        return pltpu.make_async_copy(
            mar_hbm.at[k // couplings, k % couplings], mbuf.at[k], msem.at[k])

    def amp_copy(q):
        return pltpu.make_async_copy(amp_hbm.at[q], abuf.at[q], asem.at[q])

    def scan(q, n):
        if early:
            amp_copy(q).start()
        for c in range(couplings):
            k = q * couplings + c
            slot = rel_ref[c, q] - shift
            mine = (slot >= 0) & (slot < slots)
            items[n] = k

            @pl.when(mine)
            def _():
                mar_copy(k).start()

            n = n + mine.astype(jnp.int32)
        return n

    n = lax.fori_loop(0, sources, scan, jnp.int32(0))
    for u in range(UNROLL):
        items[n + u] = items[0]

    @pl.loop(0, slots)
    def _(s):
        acc_ref[s] = jnp.zeros(acc_ref.shape[1:], F32)
        if early:
            far_ref[s] = jnp.zeros(acc_ref.shape[1:], F32)

    def wait_amp(q, x):
        amp_copy(q).wait()
        return x

    def body(g, waited):
        ks = [items[g * UNROLL + u] for u in range(UNROLL)]
        last = ks[0] // couplings
        for u in range(UNROLL):
            @pl.when(g * UNROLL + u < n)
            def _(u=u):
                mar_copy(ks[u]).wait()

            last = jnp.maximum(last, ks[u] // couplings)

        if early:
            lax.fori_loop(waited, last + 1, wait_amp, 0)
        for u in range(UNROLL):
            left = mbuf[ks[u], pl.ds(row0, rows), :]
            if early:
                left = jnp.concatenate([left, mbuf[ks[u], pl.ds(far0, rows), :]], axis=0)
            fbuf[u] = jnp.dot(
                left, abuf[ks[u] // couplings], preferred_element_type=F32).astype(BF16)
        for u in range(UNROLL):
            c, q = ks[u] % couplings, ks[u] // couplings
            weight = jnp.where(g * UNROLL + u < n, w_ref[c, q], 0.0)
            term = weight * nt_dot(fbuf[u], mbuf[ks[u]])
            acc_ref[rel_ref[c, q] - shift] += term[:rows]
            if early:
                far_ref[rel_ref[c, q] - shift] += term[rows:]
        return jnp.maximum(waited, last + 1)

    waited = lax.fori_loop(0, pl.cdiv(n, UNROLL), body, jnp.int32(0))
    if early:
        lax.fori_loop(waited, sources, wait_amp, 0)

        @pl.loop(0, slots)
        def _(s):
            early_ref[s] = acc_ref[s, :early].astype(BF16)


def coupling(meta, rel, weights, amplitudes, margins, rows, early):
    pairs, width = amplitudes.shape[0], amplitudes.shape[1]
    total = pairs * margins.shape[1]
    hbm = pl.BlockSpec(memory_space=pltpu.HBM)
    vmem = pl.BlockSpec(memory_space=VMEM)
    smem = pl.BlockSpec(memory_space=SMEM)
    out_shape = [jax.ShapeDtypeStruct((pairs, rows, width), F32)]
    scratch = [
        VMEM((total, width, width), BF16),
        VMEM((UNROLL, 2 * rows if early else rows, width), BF16),
        SMEM((total + UNROLL,), jnp.int32),
        pltpu.SemaphoreType.DMA((total,)),
    ]
    if early:
        amplitudes = pltpu.with_memory_space_constraint(amplitudes, pltpu.HBM)
        out_shape += [out_shape[0], jax.ShapeDtypeStruct((pairs, early, width), BF16)]
        scratch += [VMEM((pairs, width, width), BF16), pltpu.SemaphoreType.DMA((pairs,))]
    return pl.pallas_call(
        functools.partial(coupling_kernel, early),
        out_shape=out_shape,
        in_specs=[smem, smem, smem, hbm if early else vmem, hbm],
        out_specs=[vmem] * len(out_shape),
        scratch_shapes=scratch,
        compiler_params=pltpu.CompilerParams(vmem_limit_bytes=12 * MIB),
        cost_estimate=pl.CostEstimate(
            flops=2 * 22 * 2 * rows * 256 * 256, bytes_accessed=6 * MIB, transcendentals=0),
    )(meta, rel, weights, amplitudes, pltpu.with_memory_space_constraint(margins, pltpu.HBM))


def whole(kernel, out_shape, n_smem, n_vmem, limit, cost, **extra):
    vmem = pl.BlockSpec(memory_space=VMEM)
    return pl.pallas_call(
        kernel,
        out_shape=out_shape,
        in_specs=[pl.BlockSpec(memory_space=SMEM)] * n_smem + [vmem] * n_vmem,
        out_specs=jax.tree.map(lambda _: vmem, out_shape),
        compiler_params=pltpu.CompilerParams(vmem_limit_bytes=limit * MIB),
        cost_estimate=pl.CostEstimate(flops=cost[0], bytes_accessed=cost[1] * MIB, transcendentals=0),
        **extra,
    )


def products(far, near_blk, blk, meta_ref, prod):
    rows = prod.shape[1]
    core = meta_ref[1]
    row0 = pl.multiple_of((1 - core if far else core) * rows, rows)
    for j in range(2):
        for i in range(2):
            prod[2 * j + i] = tn_dot(near_blk[j, :, pl.ds(row0, rows)], blk[i])
    prod[4] = jnp.zeros(prod.shape[1:], F32)


def pick(meta_ref, orbs_ref, s):
    second = orbs_ref[1, s] - 2 * meta_ref[0]
    mine = (second >= 0) & (second < 2)
    return jnp.where(mine, 2 * (orbs_ref[0, s] % 2) + second, 4)


def near_kernel(meta_ref, orbs_ref, near_blk, blk, acc_ref, out, prod):
    products(False, near_blk, blk, meta_ref, prod)
    slots, early = acc_ref.shape[0], prod.shape[1] - out.shape[1]

    @pl.loop(0, slots)
    def _(s):
        out[s] = (acc_ref[s, early:] + prod[pick(meta_ref, orbs_ref, s), early:]).astype(BF16)

    for k in range(4):
        out[slots + k] = prod[k, :early].astype(BF16)


def far_kernel(meta_ref, orbs_ref, near_blk, blk, acc_ref, *rest):
    out_refs, prod = rest[:-1], rest[-1]
    products(True, near_blk, blk, meta_ref, prod)
    start = 0
    for out in out_refs:
        @pl.loop(0, out.shape[0])
        def _(s, out=out, start=start):
            out[s] = (acc_ref[start + s]
                      + prod[pick(meta_ref, orbs_ref, start + s)]).astype(BF16)

        start += out.shape[0]


def message(kernel, meta, orbs, near_blk, blk, acc, outs):
    width = acc.shape[2]
    return whole(
        kernel,
        [jax.ShapeDtypeStruct((*n, width), BF16) for n in outs],
        2, 3, 4, (4 * 2 * 128 * 256 * 1024, 4),
        scratch_shapes=[VMEM((5, width // 2, width), F32)],
    )(meta, orbs, near_blk, blk, acc)


def exchange_kernel(meta_ref, near_blk, blk, keep_ref, send_ref):
    rows = keep_ref.shape[1]
    for out, side in ((keep_ref, meta_ref[1]), (send_ref, 1 - meta_ref[1])):
        row0 = pl.multiple_of(side * rows, rows)
        for i in range(2):
            left = blk[i, :, pl.ds(row0, rows)]
            for j in range(2):
                out[2 * i + j] = tn_dot(left, near_blk[j])
                out[4 + 2 * i + j] = tn_dot(left, blk[j])


def exchange(meta, near_blk, blk):
    width = blk.shape[2]
    half = jax.ShapeDtypeStruct((8, width // 2, width), F32)
    return whole(
        exchange_kernel, [half, half], 1, 2, 4, (16 * 2 * 128 * 256 * 1024, 4),
    )(meta, near_blk, blk)


def base_kernel(meta_ref, orbs_ref, occ_ref, en_ref, amp_ref, own_ref,
                early_ref, near_ref, keep_ref, recv_ref, out_ref):
    slots, rows, width = out_ref.shape
    early = early_ref.shape[1]
    holder, core = meta_ref[0], meta_ref[1]
    row0 = pl.multiple_of(core * rows, rows)

    @pl.loop(0, slots)
    def _(p):
        first, second = orbs_ref[0, p], orbs_ref[1, p]
        side = second // 2 - holder
        step = 1 - 2 * core
        index = 2 * (first % 2) + second % 2
        both = index + jnp.where(side == 0, 4, 0)
        cols = en_ref[pl.ds(p, 1), :]
        mine = jnp.where(core == 0, cols[:, :rows], cols[:, rows:])
        down = jnp.broadcast_to(mine, (rows, rows)).T
        down = jnp.concatenate([down] * (width // rows), axis=1)
        denom = down + cols - (occ_ref[first] + occ_ref[second])
        value = denom * amp_ref[p, pl.ds(row0, rows), :].astype(F32)
        value += own_ref[p]
        value += keep_ref[both] * jnp.where(side == -step, 0.0, 1.0)
        value += recv_ref[both] * jnp.where(side == step, 0.0, 1.0)
        lacking = near_ref[slots + index].astype(F32) * jnp.where(side == -step, 1.0, 0.0)
        out_ref[p, :early] = value[:early] + early_ref[p].astype(F32) + lacking
        out_ref[p, early:] = value[early:] + near_ref[p].astype(F32)


def base(meta, orbs, occ, energy, amplitudes, own, early, near, keep, recv):
    return whole(
        base_kernel, jax.ShapeDtypeStruct(own.shape, F32), 3, 7, 4, (16 * 128 * 256 * 8, 8),
    )(meta, orbs, occ, energy, amplitudes, own, early, near, keep, recv)


def final_kernel(start, meta_ref, count_ref, base_ref, far_ref, *rest):
    out_hbm, buf, sem = rest[-3:]
    slots, rows, width = far_ref.shape
    row = lax.broadcasted_iota(jnp.int32, (rows, width), 0) + meta_ref[1] * rows
    col = lax.broadcasted_iota(jnp.int32, (rows, width), 1)
    most = jnp.maximum(row, col)

    def put(s):
        return pltpu.make_async_copy(buf.at[s], out_hbm.at[start + s], sem.at[s])

    @pl.loop(0, slots)
    def _(s):
        value = base_ref[start + s] + far_ref[s].astype(F32)
        buf[s] = jnp.where(most < count_ref[start + s], value, 0.0)
        put(s).start()

    @pl.loop(0, slots)
    def _(s):
        put(s).wait()


def final(start, meta, count, base_terms, far, earlier=None):
    slots, rows, width = far.shape
    smem = pl.BlockSpec(memory_space=SMEM)
    vmem = pl.BlockSpec(memory_space=VMEM)
    hbm = pl.BlockSpec(memory_space=pltpu.HBM)
    more = [] if earlier is None else [earlier]

    def kernel(*refs):
        final_kernel(start, *refs)

    return pl.pallas_call(
        kernel,
        out_shape=jax.ShapeDtypeStruct(base_terms.shape, F32),
        in_specs=[smem, smem, vmem, vmem] + [hbm] * len(more),
        out_specs=hbm,
        scratch_shapes=[VMEM((slots, rows, width), F32), pltpu.SemaphoreType.DMA((slots,))],
        input_output_aliases={4: 0} if more else {},
        compiler_params=pltpu.CompilerParams(vmem_limit_bytes=4 * MIB),
        cost_estimate=pl.CostEstimate(
            flops=slots * 128 * 256 * 2, bytes_accessed=slots * MIB // 4, transcendentals=0),
    )(meta, count, base_terms, far, *more)


def local(blocks, pair_orbs, pno_count, amplitudes, margins, couple_target, couple_weight,
          pno_energy, occ_energy):
    holder = lax.axis_index("pairs").astype(jnp.int32)
    core = lax.axis_index("aux").astype(jnp.int32)
    holders = lax.axis_size("pairs")
    pairs, width = amplitudes.shape[0], amplitudes.shape[1]
    straight_in = toward(holders, False, True)
    straight_out = toward(holders, False, False)
    cross_out = toward(holders, True, False)
    swap = [(2 * h + c, 2 * h + 1 - c) for h in range(holders) for c in range(2)]

    orbs = pair_orbs.T
    near_blk = lax.ppermute(blocks, AXES, straight_in)
    near_orbs = lax.ppermute(orbs, AXES, straight_in)

    meta = jnp.stack([holder, core])
    rel = lax.dynamic_slice_in_dim(couple_target, holder * pairs, pairs, 0).T - holder * pairs
    weights = lax.dynamic_slice_in_dim(couple_weight, holder * pairs, pairs, 0).T
    rows, early_rows = width // 2, width // 4
    acc_near, acc_far, msg_early = coupling(
        meta, rel, weights, amplitudes, margins, rows, early_rows)
    early = lax.ppermute(msg_early, AXES, straight_out)

    chunks = [pairs * 3 // 4, pairs - pairs * 3 // 4]
    msg_near, = message(
        near_kernel, meta, near_orbs, near_blk, blocks, acc_near,
        [(pairs + 4, rows - early_rows)])
    near = lax.ppermute(msg_near, AXES, straight_out)
    msg_far = message(
        far_kernel, meta, near_orbs, near_blk, blocks, acc_far,
        [(n, rows) for n in chunks])
    far = lax.ppermute(msg_far[0], AXES, cross_out)
    last = lax.ppermute(msg_far[1], AXES, cross_out)

    keep, send = exchange(meta, near_blk, blocks)
    recv = lax.ppermute(send, AXES, swap)
    own, = coupling(meta, rel, weights, amplitudes, margins, rows, 0)
    base_terms = base(meta, orbs, occ_energy, pno_energy, amplitudes, own, early, near,
                      keep, recv)
    out = final(0, meta, pno_count, base_terms, far)
    return final(chunks[0], meta, pno_count, base_terms, last, out)


def solution(mesh):
    placed = (
        P("pairs", "aux", None),
        P("pairs", None),
        P("pairs"),
        P("pairs", None, None),
        P("pairs", None, None, None),
        P(),
        P(),
        P("pairs", None),
        P(),
    )

    return jax.shard_map(
        local, mesh=mesh, in_specs=placed, out_specs=P("pairs", "aux", None), check_vma=False
    )
```

```python
import functools

import jax
import jax.numpy as jnp
from jax import lax
from jax.experimental import pallas as pl
from jax.experimental.pallas import tpu as pltpu
from jax.sharding import PartitionSpec as P

AXES = ("pairs", "aux")
BF16, F32 = jnp.bfloat16, jnp.float32
VMEM, SMEM = pltpu.VMEM, pltpu.SMEM
UNROLL = 4
MIB = 1 << 20


def toward(count, cross, flip):
    pairs = []
    for holder in range(count):
        for core in range(2):
            step = 1 if (core == 0) != flip else -1
            if 0 <= holder + step < count:
                dest = (1 - core) if cross else core
                pairs.append((2 * holder + core, 2 * (holder + step) + dest))
    return pairs


def nt_dot(a, b):
    return lax.dot_general(a, b, (((1,), (1,)), ((), ())), preferred_element_type=F32)


def tn_dot(a, b):
    return lax.dot_general(a, b, (((0,), (0,)), ((), ())), preferred_element_type=F32)


def sum_terms(items, n, rel_ref, w_ref, shift, mbuf, abuf, fbuf, row0s, acc_refs, ready):
    couplings, rows = rel_ref.shape[0], acc_refs[0].shape[1]
    for u in range(UNROLL):
        items[n + u] = items[0]

    @pl.loop(0, acc_refs[0].shape[0])
    def _(s):
        for acc in acc_refs:
            acc[s] = jnp.zeros(acc.shape[1:], F32)

    def body(g, carry):
        ks = [items[g * UNROLL + u] for u in range(UNROLL)]
        live = [g * UNROLL + u < n for u in range(UNROLL)]
        carry = ready(ks, live, carry)
        for u in range(UNROLL):
            parts = [mbuf[ks[u], pl.ds(row0, rows), :] for row0 in row0s]
            left = parts[0] if len(parts) == 1 else jnp.concatenate(parts, axis=0)
            fbuf[u] = jnp.dot(
                left, abuf[ks[u] // couplings], preferred_element_type=F32).astype(BF16)
        for u in range(UNROLL):
            c, q = ks[u] % couplings, ks[u] // couplings
            weight = jnp.where(live[u], w_ref[c, q], 0.0)
            term = weight * nt_dot(fbuf[u], mbuf[ks[u]])
            for k, acc in enumerate(acc_refs):
                acc[rel_ref[c, q] - shift] += term[k * rows:(k + 1) * rows]
        return carry

    return lax.fori_loop(0, pl.cdiv(n, UNROLL), body, jnp.int32(0))


def list_terms(items, rel_ref, shift, slots, found):
    couplings, sources = rel_ref.shape

    def scan(q, n):
        for c in range(couplings):
            slot = rel_ref[c, q] - shift
            mine = (slot >= 0) & (slot < slots)
            items[n] = q * couplings + c
            if found is not None:
                pl.when(mine)(functools.partial(found, q, c))
            n = n + mine.astype(jnp.int32)
        return n

    return lax.fori_loop(0, sources, scan, jnp.int32(0))


def outward_kernel(meta_ref, rel_ref, w_ref, amp_hbm, mar_hbm, near_ref, far_ref, early_ref,
                   mbuf, abuf, fbuf, items, own_items, msem, asem):
    couplings, sources = rel_ref.shape
    slots, rows, early = near_ref.shape[0], near_ref.shape[1], early_ref.shape[1]
    core = meta_ref[1]
    shift = (1 - 2 * core) * slots

    def mar_copy(k):
        return pltpu.make_async_copy(
            mar_hbm.at[k // couplings, k % couplings], mbuf.at[k], msem.at[k])

    def amp_copy(q):
        return pltpu.make_async_copy(amp_hbm.at[q], abuf.at[q], asem.at[q])

    @pl.loop(0, sources // 4)
    def _(q):
        amp_copy(q).start()

    n = list_terms(items, rel_ref, shift, slots, lambda q, c: mar_copy(q * couplings + c).start())

    @pl.loop(sources // 4, sources)
    def _(q):
        amp_copy(q).start()

    n_own = list_terms(
        own_items, rel_ref, 0, slots, lambda q, c: mar_copy(q * couplings + c).start())

    def wait_amp(q, x):
        amp_copy(q).wait()
        return x

    def ready(ks, live, waited):
        last = ks[0] // couplings
        for k, on in zip(ks, live):
            pl.when(on)(lambda k=k: mar_copy(k).wait())
            last = jnp.maximum(last, k // couplings)
        lax.fori_loop(waited, last + 1, wait_amp, 0)
        return jnp.maximum(waited, last + 1)

    row0s = [pl.multiple_of(core * rows, rows), pl.multiple_of(rows - core * rows, rows)]
    waited = sum_terms(
        items, n, rel_ref, w_ref, shift, mbuf, abuf, fbuf, row0s, [near_ref, far_ref], ready)

    @pl.loop(0, slots)
    def _(s):
        early_ref[s] = near_ref[s, :early].astype(BF16)

    lax.fori_loop(waited, sources, wait_amp, 0)

    @pl.loop(0, n_own)
    def _(i):
        mar_copy(own_items[i]).wait()


def own_kernel(meta_ref, rel_ref, w_ref, abuf, mbuf, acc_ref, fbuf, items):
    slots, rows = acc_ref.shape[0], acc_ref.shape[1]
    n = list_terms(items, rel_ref, 0, slots, None)
    sum_terms(items, n, rel_ref, w_ref, 0, mbuf, abuf, fbuf,
              [pl.multiple_of(meta_ref[1] * rows, rows)], [acc_ref], lambda ks, live, c: c)


def outward(meta, rel, weights, amplitudes, margins, rows, early):
    pairs, width = amplitudes.shape[0], amplitudes.shape[1]
    total = pairs * margins.shape[1]
    hbm = pl.BlockSpec(memory_space=pltpu.HBM)
    vmem = pl.BlockSpec(memory_space=VMEM)
    smem = pl.BlockSpec(memory_space=SMEM)
    half = jax.ShapeDtypeStruct((pairs, rows, width), F32)
    return pl.pallas_call(
        outward_kernel,
        out_shape=[
            half, half,
            jax.ShapeDtypeStruct((pairs, early, width), BF16),
            jax.ShapeDtypeStruct((total, width, width), BF16),
            jax.ShapeDtypeStruct((pairs, width, width), BF16),
        ],
        in_specs=[smem, smem, smem, hbm, hbm],
        out_specs=[vmem] * 5,
        scratch_shapes=[
            VMEM((UNROLL, width, width), BF16),
            SMEM((total + UNROLL,), jnp.int32),
            SMEM((total + UNROLL,), jnp.int32),
            pltpu.SemaphoreType.DMA((total,)),
            pltpu.SemaphoreType.DMA((pairs,)),
        ],
        compiler_params=pltpu.CompilerParams(vmem_limit_bytes=4 * MIB),
        cost_estimate=pl.CostEstimate(
            flops=2 * 22 * 2 * 256 * 256 * 256, bytes_accessed=8 * MIB, transcendentals=0),
        name="outward",
    )(meta, rel, weights, pltpu.with_memory_space_constraint(amplitudes, pltpu.HBM),
      pltpu.with_memory_space_constraint(margins, pltpu.HBM))


def whole(kernel, out_shape, n_smem, n_vmem, limit, cost, **extra):
    vmem = pl.BlockSpec(memory_space=VMEM)
    return pl.pallas_call(
        kernel,
        out_shape=out_shape,
        in_specs=[pl.BlockSpec(memory_space=SMEM)] * n_smem + [vmem] * n_vmem,
        out_specs=jax.tree.map(lambda _: vmem, out_shape),
        compiler_params=pltpu.CompilerParams(vmem_limit_bytes=limit * MIB),
        cost_estimate=pl.CostEstimate(flops=cost[0], bytes_accessed=cost[1] * MIB, transcendentals=0),
        **extra,
    )


def products(far, near_blk, blk, meta_ref, prod):
    rows = prod.shape[1]
    core = meta_ref[1]
    row0 = pl.multiple_of((1 - core if far else core) * rows, rows)
    for j in range(2):
        for i in range(2):
            prod[2 * j + i] = tn_dot(near_blk[j, :, pl.ds(row0, rows)], blk[i])
    prod[4] = jnp.zeros(prod.shape[1:], F32)


def pick(meta_ref, orbs_ref, s):
    second = orbs_ref[1, s] - 2 * meta_ref[0]
    mine = (second >= 0) & (second < 2)
    return jnp.where(mine, 2 * (orbs_ref[0, s] % 2) + second, 4)


def near_kernel(meta_ref, orbs_ref, near_blk, blk, acc_ref, out, prod):
    products(False, near_blk, blk, meta_ref, prod)
    slots, early = acc_ref.shape[0], out.shape[1]
    parts = prod.shape[1] // early - 1

    @pl.loop(0, slots)
    def _(s):
        value = acc_ref[s, early:] + prod[pick(meta_ref, orbs_ref, s), early:]
        out[pl.ds(parts * s, parts)] = value.astype(BF16).reshape(parts, early, -1)

    for k in range(4):
        out[parts * slots + k] = prod[k, :early].astype(BF16)


def far_kernel(meta_ref, orbs_ref, near_blk, blk, acc_ref, *rest):
    out_refs, prod = rest[:-1], rest[-1]
    products(True, near_blk, blk, meta_ref, prod)
    start = 0
    for out in out_refs:
        @pl.loop(0, out.shape[0])
        def _(s, out=out, start=start):
            out[s] = (acc_ref[start + s]
                      + prod[pick(meta_ref, orbs_ref, start + s)]).astype(BF16)

        start += out.shape[0]


def message(kernel, meta, orbs, near_blk, blk, acc, outs):
    width = acc.shape[2]
    return whole(
        kernel,
        [jax.ShapeDtypeStruct((*n, width), BF16) for n in outs],
        2, 3, 4, (4 * 2 * 128 * 256 * 1024, 4),
        scratch_shapes=[VMEM((5, width // 2, width), F32)],
    )(meta, orbs, near_blk, blk, acc)


def exchange_kernel(meta_ref, near_blk, blk, keep_ref, send_ref):
    rows = keep_ref.shape[1]
    for out, side in ((keep_ref, meta_ref[1]), (send_ref, 1 - meta_ref[1])):
        row0 = pl.multiple_of(side * rows, rows)
        for i in range(2):
            left = blk[i, :, pl.ds(row0, rows)]
            for j in range(2):
                out[2 * i + j] = tn_dot(left, near_blk[j])
                out[4 + 2 * i + j] = tn_dot(left, blk[j])


def exchange(meta, near_blk, blk):
    width = blk.shape[2]
    half = jax.ShapeDtypeStruct((8, width // 2, width), F32)
    return whole(
        exchange_kernel, [half, half], 1, 2, 4, (16 * 2 * 128 * 256 * 1024, 4),
    )(meta, near_blk, blk)


def base_kernel(meta_ref, orbs_ref, occ_ref, en_ref, amp_ref, own_ref,
                early_ref, near_ref, keep_ref, recv_ref, out_ref):
    slots, rows, width = out_ref.shape
    early = early_ref.shape[1]
    parts = rows // early - 1
    holder, core = meta_ref[0], meta_ref[1]
    row0 = pl.multiple_of(core * rows, rows)

    @pl.loop(0, slots)
    def _(p):
        first, second = orbs_ref[0, p], orbs_ref[1, p]
        side = second // 2 - holder
        step = 1 - 2 * core
        index = 2 * (first % 2) + second % 2
        both = index + jnp.where(side == 0, 4, 0)
        cols = en_ref[pl.ds(p, 1), :]
        mine = jnp.where(core == 0, cols[:, :rows], cols[:, rows:])
        down = jnp.broadcast_to(mine, (rows, rows)).T
        down = jnp.concatenate([down] * (width // rows), axis=1)
        denom = down + cols - (occ_ref[first] + occ_ref[second])
        value = denom * amp_ref[p, pl.ds(row0, rows), :].astype(F32)
        value += own_ref[p]
        value += keep_ref[both] * jnp.where(side == -step, 0.0, 1.0)
        value += recv_ref[both] * jnp.where(side == step, 0.0, 1.0)
        lacking = near_ref[parts * slots + index].astype(F32) * jnp.where(side == -step, 1.0, 0.0)
        out_ref[p, :early] = value[:early] + early_ref[p].astype(F32) + lacking
        late = near_ref[pl.ds(parts * p, parts)].reshape(rows - early, width)
        out_ref[p, early:] = value[early:] + late.astype(F32)


def base(meta, orbs, occ, energy, amplitudes, own, early, near, keep, recv):
    return whole(
        base_kernel, jax.ShapeDtypeStruct(own.shape, F32), 3, 7, 4, (16 * 128 * 256 * 8, 8),
    )(meta, orbs, occ, energy, amplitudes, own, early, near, keep, recv)


def final_kernel(start, meta_ref, count_ref, base_ref, far_ref, *rest):
    out_hbm, buf, sem = rest[-3:]
    slots, rows, width = far_ref.shape
    row = lax.broadcasted_iota(jnp.int32, (rows, width), 0) + meta_ref[1] * rows
    col = lax.broadcasted_iota(jnp.int32, (rows, width), 1)
    most = jnp.maximum(row, col)

    def put(s):
        return pltpu.make_async_copy(buf.at[s], out_hbm.at[start + s], sem.at[s])

    @pl.loop(0, slots)
    def _(s):
        value = base_ref[start + s] + far_ref[s].astype(F32)
        buf[s] = jnp.where(most < count_ref[start + s], value, 0.0)
        put(s).start()

    @pl.loop(0, slots)
    def _(s):
        put(s).wait()


def final(start, meta, count, base_terms, far, earlier=None):
    slots, rows, width = far.shape
    smem = pl.BlockSpec(memory_space=SMEM)
    vmem = pl.BlockSpec(memory_space=VMEM)
    hbm = pl.BlockSpec(memory_space=pltpu.HBM)
    more = [] if earlier is None else [earlier]

    def kernel(*refs):
        final_kernel(start, *refs)

    return pl.pallas_call(
        kernel,
        out_shape=jax.ShapeDtypeStruct(base_terms.shape, F32),
        in_specs=[smem, smem, vmem, vmem] + [hbm] * len(more),
        out_specs=hbm,
        scratch_shapes=[VMEM((slots, rows, width), F32), pltpu.SemaphoreType.DMA((slots,))],
        input_output_aliases={4: 0} if more else {},
        compiler_params=pltpu.CompilerParams(vmem_limit_bytes=4 * MIB),
        cost_estimate=pl.CostEstimate(
            flops=slots * 128 * 256 * 2, bytes_accessed=slots * MIB // 4, transcendentals=0),
    )(meta, count, base_terms, far, *more)


def local(blocks, pair_orbs, pno_count, amplitudes, margins, couple_target, couple_weight,
          pno_energy, occ_energy):
    holder = lax.axis_index("pairs").astype(jnp.int32)
    core = lax.axis_index("aux").astype(jnp.int32)
    holders = lax.axis_size("pairs")
    pairs, width = amplitudes.shape[0], amplitudes.shape[1]
    straight_in = toward(holders, False, True)
    straight_out = toward(holders, False, False)
    cross_out = toward(holders, True, False)
    swap = [(2 * h + c, 2 * h + 1 - c) for h in range(holders) for c in range(2)]

    orbs = pair_orbs.T
    near_blk = lax.ppermute(blocks, AXES, straight_in)
    near_orbs = lax.ppermute(orbs, AXES, straight_in)

    meta = jnp.stack([holder, core])
    rel = lax.dynamic_slice_in_dim(couple_target, holder * pairs, pairs, 0).T - holder * pairs
    weights = lax.dynamic_slice_in_dim(couple_weight, holder * pairs, pairs, 0).T
    rows, early_rows = width // 2, width // 8
    acc_near, acc_far, msg_early, held_mar, held_amp = outward(
        meta, rel, weights, amplitudes, margins, rows, early_rows)
    early = lax.ppermute(msg_early, AXES, straight_out)

    chunks = [pairs * 3 // 4, pairs - pairs * 3 // 4]
    msg_near, = message(
        near_kernel, meta, near_orbs, near_blk, blocks, acc_near,
        [(pairs * (rows // early_rows - 1) + 4, early_rows)])
    near = lax.ppermute(msg_near, AXES, straight_out)
    msg_far = message(
        far_kernel, meta, near_orbs, near_blk, blocks, acc_far,
        [(n, rows) for n in chunks])
    far = lax.ppermute(msg_far[0], AXES, cross_out)
    last = lax.ppermute(msg_far[1], AXES, cross_out)

    keep, send = exchange(meta, near_blk, blocks)
    recv = lax.ppermute(send, AXES, swap)
    own = whole(
        own_kernel, jax.ShapeDtypeStruct((pairs, rows, width), F32), 3, 2, 4,
        (2 * 22 * 2 * rows * 256 * 256, 4),
        scratch_shapes=[VMEM((UNROLL, rows, width), BF16),
                        SMEM((held_mar.shape[0] + UNROLL,), jnp.int32)],
    )(meta, rel, weights, held_amp, held_mar)
    base_terms = base(meta, orbs, occ_energy, pno_energy, held_amp, own, early, near,
                      keep, recv)
    out = final(0, meta, pno_count, base_terms, far)
    return final(chunks[0], meta, pno_count, base_terms, last, out)


def solution(mesh):
    placed = (
        P("pairs", "aux", None),
        P("pairs", None),
        P("pairs"),
        P("pairs", None, None),
        P("pairs", None, None, None),
        P(),
        P(),
        P("pairs", None),
        P(),
    )

    return jax.shard_map(
        local, mesh=mesh, in_specs=placed, out_specs=P("pairs", "aux", None), check_vma=False
    )
```

```python
import functools

import jax
import jax.numpy as jnp
from jax import lax
from jax.experimental import pallas as pl
from jax.experimental.pallas import tpu as pltpu
from jax.sharding import PartitionSpec as P

AXES = ("pairs", "aux")
BF16, F32 = jnp.bfloat16, jnp.float32
VMEM, SMEM = pltpu.VMEM, pltpu.SMEM
UNROLL = 4
MIB = 1 << 20


def toward(count, cross, flip):
    pairs = []
    for holder in range(count):
        for core in range(2):
            step = 1 if (core == 0) != flip else -1
            if 0 <= holder + step < count:
                dest = (1 - core) if cross else core
                pairs.append((2 * holder + core, 2 * (holder + step) + dest))
    return pairs


def nt_dot(a, b):
    return lax.dot_general(a, b, (((1,), (1,)), ((), ())), preferred_element_type=F32)


def tn_dot(a, b):
    return lax.dot_general(a, b, (((0,), (0,)), ((), ())), preferred_element_type=F32)


def coupling_kernel(early, meta_ref, rel_ref, w_ref, amp_hbm, mar_hbm, *rest):
    if early:
        far_ref, early_ref, mbuf, fbuf, items, msem, abuf, asem, acc_ref = rest
    else:
        (acc_ref, mbuf, fbuf, items, msem), abuf = rest, amp_hbm
    sources, couplings = mar_hbm.shape[0], mar_hbm.shape[1]
    slots, rows = acc_ref.shape[0], acc_ref.shape[1]
    core = meta_ref[1]
    shift = (1 - 2 * core) * slots if early else 0
    row0 = pl.multiple_of(core * rows, rows)
    far0 = pl.multiple_of(rows - core * rows, rows)

    def mar_copy(k):
        return pltpu.make_async_copy(
            mar_hbm.at[k // couplings, k % couplings], mbuf.at[k], msem.at[k])

    def amp_copy(q):
        return pltpu.make_async_copy(amp_hbm.at[q], abuf.at[q], asem.at[q])

    def scan(q, n):
        if early:
            amp_copy(q).start()
        for c in range(couplings):
            k = q * couplings + c
            slot = rel_ref[c, q] - shift
            mine = (slot >= 0) & (slot < slots)
            items[n] = k

            @pl.when(mine)
            def _():
                mar_copy(k).start()

            n = n + mine.astype(jnp.int32)
        return n

    n = lax.fori_loop(0, sources, scan, jnp.int32(0))
    for u in range(UNROLL):
        items[n + u] = items[0]

    @pl.loop(0, slots)
    def _(s):
        acc_ref[s] = jnp.zeros(acc_ref.shape[1:], F32)
        if early:
            far_ref[s] = jnp.zeros(acc_ref.shape[1:], F32)

    def wait_amp(q, x):
        amp_copy(q).wait()
        return x

    def body(g, waited):
        ks = [items[g * UNROLL + u] for u in range(UNROLL)]
        last = ks[0] // couplings
        for u in range(UNROLL):
            @pl.when(g * UNROLL + u < n)
            def _(u=u):
                mar_copy(ks[u]).wait()

            last = jnp.maximum(last, ks[u] // couplings)

        if early:
            lax.fori_loop(waited, last + 1, wait_amp, 0)
        for u in range(UNROLL):
            left = mbuf[ks[u], pl.ds(row0, rows), :]
            if early:
                left = jnp.concatenate([left, mbuf[ks[u], pl.ds(far0, rows), :]], axis=0)
            fbuf[u] = jnp.dot(
                left, abuf[ks[u] // couplings], preferred_element_type=F32).astype(BF16)
        for u in range(UNROLL):
            c, q = ks[u] % couplings, ks[u] // couplings
            weight = jnp.where(g * UNROLL + u < n, w_ref[c, q], 0.0)
            term = weight * nt_dot(fbuf[u], mbuf[ks[u]])
            acc_ref[rel_ref[c, q] - shift] += term[:rows]
            if early:
                far_ref[rel_ref[c, q] - shift] += term[rows:]
        return jnp.maximum(waited, last + 1)

    waited = lax.fori_loop(0, pl.cdiv(n, UNROLL), body, jnp.int32(0))
    if early:
        lax.fori_loop(waited, sources, wait_amp, 0)

        @pl.loop(0, slots)
        def _(s):
            early_ref[s] = acc_ref[s, :early].astype(BF16)


def coupling(meta, rel, weights, amplitudes, margins, rows, early):
    pairs, width = amplitudes.shape[0], amplitudes.shape[1]
    total = pairs * margins.shape[1]
    hbm = pl.BlockSpec(memory_space=pltpu.HBM)
    vmem = pl.BlockSpec(memory_space=VMEM)
    smem = pl.BlockSpec(memory_space=SMEM)
    out_shape = [jax.ShapeDtypeStruct((pairs, rows, width), F32)]
    scratch = [
        VMEM((total, width, width), BF16),
        VMEM((UNROLL, 2 * rows if early else rows, width), BF16),
        SMEM((total + UNROLL,), jnp.int32),
        pltpu.SemaphoreType.DMA((total,)),
    ]
    if early:
        amplitudes = pltpu.with_memory_space_constraint(amplitudes, pltpu.HBM)
        out_shape.append(jax.ShapeDtypeStruct((pairs, early, width), BF16))
        scratch += [VMEM((pairs, width, width), BF16), pltpu.SemaphoreType.DMA((pairs,)),
                    VMEM((pairs, rows, width), F32)]
    return pl.pallas_call(
        functools.partial(coupling_kernel, early),
        out_shape=out_shape,
        in_specs=[smem, smem, smem, hbm if early else vmem, hbm],
        out_specs=[vmem] * len(out_shape),
        scratch_shapes=scratch,
        compiler_params=pltpu.CompilerParams(vmem_limit_bytes=14 * MIB),
        cost_estimate=pl.CostEstimate(
            flops=2 * 22 * 2 * rows * 256 * 256, bytes_accessed=6 * MIB, transcendentals=0),
    )(meta, rel, weights, amplitudes, pltpu.with_memory_space_constraint(margins, pltpu.HBM))


def whole(kernel, out_shape, n_smem, n_vmem, limit, cost, **extra):
    vmem = pl.BlockSpec(memory_space=VMEM)
    return pl.pallas_call(
        kernel,
        out_shape=out_shape,
        in_specs=[pl.BlockSpec(memory_space=SMEM)] * n_smem + [vmem] * n_vmem,
        out_specs=jax.tree.map(lambda _: vmem, out_shape),
        compiler_params=pltpu.CompilerParams(vmem_limit_bytes=limit * MIB),
        cost_estimate=pl.CostEstimate(flops=cost[0], bytes_accessed=cost[1] * MIB, transcendentals=0),
        **extra,
    )


def products(far, near_blk, blk, meta_ref, prod):
    rows = prod.shape[1]
    core = meta_ref[1]
    row0 = pl.multiple_of((1 - core if far else core) * rows, rows)
    for j in range(2):
        for i in range(2):
            prod[2 * j + i] = tn_dot(near_blk[j, :, pl.ds(row0, rows)], blk[i])
    prod[4] = jnp.zeros(prod.shape[1:], F32)


def pick(meta_ref, orbs_ref, s):
    second = orbs_ref[1, s] - 2 * meta_ref[0]
    mine = (second >= 0) & (second < 2)
    return jnp.where(mine, 2 * (orbs_ref[0, s] % 2) + second, 4)


def near_kernel(meta_ref, near_blk, blk, out, prod):
    products(False, near_blk, blk, meta_ref, prod)
    for k in range(4):
        out[k] = prod[k].astype(BF16)


def far_kernel(meta_ref, orbs_ref, near_blk, blk, acc_ref, *rest):
    out_refs, prod = rest[:-1], rest[-1]
    products(True, near_blk, blk, meta_ref, prod)
    start = 0
    for out in out_refs:
        @pl.loop(0, out.shape[0])
        def _(s, out=out, start=start):
            out[s] = (acc_ref[start + s]
                      + prod[pick(meta_ref, orbs_ref, start + s)]).astype(BF16)

        start += out.shape[0]


def message(kernel, smem, vmem, outs, width):
    return whole(
        kernel,
        [jax.ShapeDtypeStruct((*n, width), BF16) for n in outs],
        len(smem), len(vmem), 4, (4 * 2 * 128 * 256 * 1024, 4),
        scratch_shapes=[VMEM((5, width // 2, width), F32)],
    )(*smem, *vmem)


def exchange_kernel(meta_ref, near_blk, blk, keep_ref, send_ref):
    rows = keep_ref.shape[1]
    for out, side in ((keep_ref, meta_ref[1]), (send_ref, 1 - meta_ref[1])):
        row0 = pl.multiple_of(side * rows, rows)
        for i in range(2):
            left = blk[i, :, pl.ds(row0, rows)]
            for j in range(2):
                out[2 * i + j] = tn_dot(left, near_blk[j])
                out[4 + 2 * i + j] = tn_dot(left, blk[j])


def exchange(meta, near_blk, blk):
    width = blk.shape[2]
    half = jax.ShapeDtypeStruct((8, width // 2, width), F32)
    return whole(
        exchange_kernel, [half, half], 1, 2, 4, (16 * 2 * 128 * 256 * 1024, 4),
    )(meta, near_blk, blk)


def base_kernel(meta_ref, orbs_ref, occ_ref, en_ref, amp_ref, own_ref,
                early_ref, near_ref, keep_ref, recv_ref, out_ref):
    slots, rows, width = out_ref.shape
    holder, core = meta_ref[0], meta_ref[1]
    row0 = pl.multiple_of(core * rows, rows)

    @pl.loop(0, slots)
    def _(p):
        first, second = orbs_ref[0, p], orbs_ref[1, p]
        side = second // 2 - holder
        step = 1 - 2 * core
        index = 2 * (first % 2) + second % 2
        both = index + jnp.where(side == 0, 4, 0)
        cols = en_ref[pl.ds(p, 1), :]
        mine = jnp.where(core == 0, cols[:, :rows], cols[:, rows:])
        down = jnp.broadcast_to(mine, (rows, rows)).T
        down = jnp.concatenate([down] * (width // rows), axis=1)
        denom = down + cols - (occ_ref[first] + occ_ref[second])
        value = denom * amp_ref[p, pl.ds(row0, rows), :].astype(F32)
        value += own_ref[p]
        value += keep_ref[both] * jnp.where(side == -step, 0.0, 1.0)
        value += recv_ref[both] * jnp.where(side == step, 0.0, 1.0)
        value += near_ref[index].astype(F32) * jnp.where(side == -step, 1.0, 0.0)
        out_ref[p] = value + early_ref[p].astype(F32)


def base(meta, orbs, occ, energy, amplitudes, own, early, near, keep, recv):
    return whole(
        base_kernel, jax.ShapeDtypeStruct(own.shape, F32), 3, 7, 4, (16 * 128 * 256 * 8, 8),
    )(meta, orbs, occ, energy, amplitudes, own, early, near, keep, recv)


def final_kernel(start, meta_ref, count_ref, base_ref, far_ref, *rest):
    out_hbm, buf, sem = rest[-3:]
    slots, rows, width = far_ref.shape
    row = lax.broadcasted_iota(jnp.int32, (rows, width), 0) + meta_ref[1] * rows
    col = lax.broadcasted_iota(jnp.int32, (rows, width), 1)
    most = jnp.maximum(row, col)

    def put(s):
        return pltpu.make_async_copy(buf.at[s], out_hbm.at[start + s], sem.at[s])

    @pl.loop(0, slots)
    def _(s):
        value = base_ref[start + s] + far_ref[s].astype(F32)
        buf[s] = jnp.where(most < count_ref[start + s], value, 0.0)
        put(s).start()

    @pl.loop(0, slots)
    def _(s):
        put(s).wait()


def final(start, meta, count, base_terms, far, earlier=None):
    slots, rows, width = far.shape
    smem = pl.BlockSpec(memory_space=SMEM)
    vmem = pl.BlockSpec(memory_space=VMEM)
    hbm = pl.BlockSpec(memory_space=pltpu.HBM)
    more = [] if earlier is None else [earlier]

    def kernel(*refs):
        final_kernel(start, *refs)

    return pl.pallas_call(
        kernel,
        out_shape=jax.ShapeDtypeStruct(base_terms.shape, F32),
        in_specs=[smem, smem, vmem, vmem] + [hbm] * len(more),
        out_specs=hbm,
        scratch_shapes=[VMEM((slots, rows, width), F32), pltpu.SemaphoreType.DMA((slots,))],
        input_output_aliases={4: 0} if more else {},
        compiler_params=pltpu.CompilerParams(vmem_limit_bytes=4 * MIB),
        cost_estimate=pl.CostEstimate(
            flops=slots * 128 * 256 * 2, bytes_accessed=slots * MIB // 4, transcendentals=0),
    )(meta, count, base_terms, far, *more)


def local(blocks, pair_orbs, pno_count, amplitudes, margins, couple_target, couple_weight,
          pno_energy, occ_energy):
    holder = lax.axis_index("pairs").astype(jnp.int32)
    core = lax.axis_index("aux").astype(jnp.int32)
    holders = lax.axis_size("pairs")
    pairs, width = amplitudes.shape[0], amplitudes.shape[1]
    straight_in = toward(holders, False, True)
    straight_out = toward(holders, False, False)
    cross_out = toward(holders, True, False)
    swap = [(2 * h + c, 2 * h + 1 - c) for h in range(holders) for c in range(2)]

    orbs = pair_orbs.T
    near_blk = lax.ppermute(blocks, AXES, straight_in)
    near_orbs = lax.ppermute(orbs, AXES, straight_in)

    meta = jnp.stack([holder, core])
    rel = lax.dynamic_slice_in_dim(couple_target, holder * pairs, pairs, 0).T - holder * pairs
    weights = lax.dynamic_slice_in_dim(couple_weight, holder * pairs, pairs, 0).T
    rows = width // 2
    acc_far, msg_early = coupling(
        meta, rel, weights, amplitudes, margins, rows, rows)
    early = lax.ppermute(msg_early, AXES, straight_out)

    chunks = [pairs * 3 // 4, pairs - pairs * 3 // 4]
    msg_near, = message(
        near_kernel, [meta], [near_blk, blocks], [(4, rows)], width)
    near = lax.ppermute(msg_near, AXES, straight_out)
    msg_far = message(
        far_kernel, [meta, near_orbs], [near_blk, blocks, acc_far],
        [(n, rows) for n in chunks], width)
    far = lax.ppermute(msg_far[0], AXES, cross_out)
    last = lax.ppermute(msg_far[1], AXES, cross_out)

    keep, send = exchange(meta, near_blk, blocks)
    recv = lax.ppermute(send, AXES, swap)
    own, = coupling(meta, rel, weights, amplitudes, margins, rows, 0)
    base_terms = base(meta, orbs, occ_energy, pno_energy, amplitudes, own, early, near,
                      keep, recv)
    out = final(0, meta, pno_count, base_terms, far)
    return final(chunks[0], meta, pno_count, base_terms, last, out)


def solution(mesh):
    placed = (
        P("pairs", "aux", None),
        P("pairs", None),
        P("pairs"),
        P("pairs", None, None),
        P("pairs", None, None, None),
        P(),
        P(),
        P("pairs", None),
        P(),
    )

    return jax.shard_map(
        local, mesh=mesh, in_specs=placed, out_specs=P("pairs", "aux", None), check_vma=False
    )
```

```python
import functools

import jax
import jax.numpy as jnp
from jax import lax
from jax.experimental import pallas as pl
from jax.experimental.pallas import tpu as pltpu
from jax.sharding import PartitionSpec as P

AXES = ("pairs", "aux")
BF16, F32 = jnp.bfloat16, jnp.float32
VMEM, SMEM = pltpu.VMEM, pltpu.SMEM
UNROLL = 4
MIB = 1 << 20


def toward(count, cross, flip):
    pairs = []
    for holder in range(count):
        for core in range(2):
            step = 1 if (core == 0) != flip else -1
            if 0 <= holder + step < count:
                dest = (1 - core) if cross else core
                pairs.append((2 * holder + core, 2 * (holder + step) + dest))
    return pairs


def nt_dot(a, b):
    return lax.dot_general(a, b, (((1,), (1,)), ((), ())), preferred_element_type=F32)


def tn_dot(a, b):
    return lax.dot_general(a, b, (((0,), (0,)), ((), ())), preferred_element_type=F32)


def coupling_kernel(early, meta_ref, rel_ref, w_ref, amp_hbm, mar_hbm, *rest):
    if early:
        far_ref, early_ref, mbuf, fbuf, items, msem, abuf, asem, acc_ref = rest
    else:
        (acc_ref, mbuf, fbuf, items, msem), abuf = rest, amp_hbm
    sources, couplings = mar_hbm.shape[0], mar_hbm.shape[1]
    slots, rows = acc_ref.shape[0], acc_ref.shape[1]
    core = meta_ref[1]
    shift = (1 - 2 * core) * slots if early else 0
    row0 = pl.multiple_of(core * rows, rows)
    far0 = pl.multiple_of(rows - core * rows, rows)

    def mar_copy(k):
        return pltpu.make_async_copy(
            mar_hbm.at[k // couplings, k % couplings], mbuf.at[k], msem.at[k])

    def amp_copy(q):
        return pltpu.make_async_copy(amp_hbm.at[q], abuf.at[q], asem.at[q])

    def scan(q, n):
        if early:
            amp_copy(q).start()
        for c in range(couplings):
            k = q * couplings + c
            slot = rel_ref[c, q] - shift
            mine = (slot >= 0) & (slot < slots)
            items[n] = k

            @pl.when(mine)
            def _():
                mar_copy(k).start()

            n = n + mine.astype(jnp.int32)
        return n

    n = lax.fori_loop(0, sources, scan, jnp.int32(0))
    for u in range(UNROLL):
        items[n + u] = items[0]

    @pl.loop(0, slots)
    def _(s):
        acc_ref[s] = jnp.zeros(acc_ref.shape[1:], F32)
        if early:
            far_ref[s] = jnp.zeros(acc_ref.shape[1:], F32)

    def wait_amp(q, x):
        amp_copy(q).wait()
        return x

    def body(g, waited):
        ks = [items[g * UNROLL + u] for u in range(UNROLL)]
        last = ks[0] // couplings
        for u in range(UNROLL):
            @pl.when(g * UNROLL + u < n)
            def _(u=u):
                mar_copy(ks[u]).wait()

            last = jnp.maximum(last, ks[u] // couplings)

        if early:
            lax.fori_loop(waited, last + 1, wait_amp, 0)
        for u in range(UNROLL):
            left = mbuf[ks[u], pl.ds(row0, rows), :]
            if early:
                left = jnp.concatenate([left, mbuf[ks[u], pl.ds(far0, rows), :]], axis=0)
            fbuf[u] = jnp.dot(
                left, abuf[ks[u] // couplings], preferred_element_type=F32).astype(BF16)
        for u in range(UNROLL):
            c, q = ks[u] % couplings, ks[u] // couplings
            weight = jnp.where(g * UNROLL + u < n, w_ref[c, q], 0.0)
            term = weight * nt_dot(fbuf[u], mbuf[ks[u]])
            acc_ref[rel_ref[c, q] - shift] += term[:rows]
            if early:
                far_ref[rel_ref[c, q] - shift] += term[rows:]
        return jnp.maximum(waited, last + 1)

    waited = lax.fori_loop(0, pl.cdiv(n, UNROLL), body, jnp.int32(0))
    if early:
        lax.fori_loop(waited, sources, wait_amp, 0)

        @pl.loop(0, slots)
        def _(s):
            early_ref[s] = acc_ref[s, :early].astype(BF16)


def coupling(meta, rel, weights, amplitudes, margins, rows, early):
    pairs, width = amplitudes.shape[0], amplitudes.shape[1]
    total = pairs * margins.shape[1]
    hbm = pl.BlockSpec(memory_space=pltpu.HBM)
    vmem = pl.BlockSpec(memory_space=VMEM)
    smem = pl.BlockSpec(memory_space=SMEM)
    out_shape = [jax.ShapeDtypeStruct((pairs, rows, width), F32)]
    scratch = [
        VMEM((total, width, width), BF16),
        VMEM((UNROLL, 2 * rows if early else rows, width), BF16),
        SMEM((total + UNROLL,), jnp.int32),
        pltpu.SemaphoreType.DMA((total,)),
    ]
    if early:
        amplitudes = pltpu.with_memory_space_constraint(amplitudes, pltpu.HBM)
        out_shape.append(jax.ShapeDtypeStruct((pairs, early, width), BF16))
        scratch += [VMEM((pairs, width, width), BF16), pltpu.SemaphoreType.DMA((pairs,)),
                    VMEM((pairs, rows, width), F32)]
    return pl.pallas_call(
        functools.partial(coupling_kernel, early),
        out_shape=out_shape,
        in_specs=[smem, smem, smem, hbm if early else vmem, hbm],
        out_specs=[vmem] * len(out_shape),
        scratch_shapes=scratch,
        compiler_params=pltpu.CompilerParams(vmem_limit_bytes=14 * MIB),
        cost_estimate=pl.CostEstimate(
            flops=2 * 22 * 2 * rows * 256 * 256, bytes_accessed=6 * MIB, transcendentals=0),
    )(meta, rel, weights, amplitudes, pltpu.with_memory_space_constraint(margins, pltpu.HBM))


def whole(kernel, out_shape, n_smem, n_vmem, limit, cost, **extra):
    vmem = pl.BlockSpec(memory_space=VMEM)
    return pl.pallas_call(
        kernel,
        out_shape=out_shape,
        in_specs=[pl.BlockSpec(memory_space=SMEM)] * n_smem + [vmem] * n_vmem,
        out_specs=jax.tree.map(lambda _: vmem, out_shape),
        compiler_params=pltpu.CompilerParams(vmem_limit_bytes=limit * MIB),
        cost_estimate=pl.CostEstimate(flops=cost[0], bytes_accessed=cost[1] * MIB, transcendentals=0),
        **extra,
    )


def products(far, near_blk, blk, meta_ref, prod):
    rows = prod.shape[1]
    core = meta_ref[1]
    row0 = pl.multiple_of((1 - core if far else core) * rows, rows)
    for j in range(2):
        for i in range(2):
            prod[2 * j + i] = tn_dot(near_blk[j, :, pl.ds(row0, rows)], blk[i])
    prod[4] = jnp.zeros(prod.shape[1:], F32)


def pick(meta_ref, orbs_ref, s):
    second = orbs_ref[1, s] - 2 * meta_ref[0]
    mine = (second >= 0) & (second < 2)
    return jnp.where(mine, 2 * (orbs_ref[0, s] % 2) + second, 4)


def near_kernel(meta_ref, near_blk, blk, out, prod):
    products(False, near_blk, blk, meta_ref, prod)
    for k in range(4):
        out[k] = prod[k].astype(BF16)


def far_kernel(meta_ref, orbs_ref, near_blk, blk, acc_ref, *rest):
    out_refs, prod = rest[:-1], rest[-1]
    products(True, near_blk, blk, meta_ref, prod)
    start = 0
    for out in out_refs:
        @pl.loop(0, out.shape[0])
        def _(s, out=out, start=start):
            out[s] = (acc_ref[start + s]
                      + prod[pick(meta_ref, orbs_ref, start + s)]).astype(BF16)

        start += out.shape[0]


def message(kernel, smem, vmem, outs, width):
    return whole(
        kernel,
        [jax.ShapeDtypeStruct((*n, width), BF16) for n in outs],
        len(smem), len(vmem), 4, (4 * 2 * 128 * 256 * 1024, 4),
        scratch_shapes=[VMEM((5, width // 2, width), F32)],
    )(*smem, *vmem)


def exchange_kernel(meta_ref, near_blk, blk, keep_ref, send_ref):
    rows = keep_ref.shape[1]
    for out, side in ((keep_ref, meta_ref[1]), (send_ref, 1 - meta_ref[1])):
        row0 = pl.multiple_of(side * rows, rows)
        for i in range(2):
            left = blk[i, :, pl.ds(row0, rows)]
            for j in range(2):
                out[2 * i + j] = tn_dot(left, near_blk[j])
                out[4 + 2 * i + j] = tn_dot(left, blk[j])


def exchange(meta, near_blk, blk):
    width = blk.shape[2]
    half = jax.ShapeDtypeStruct((8, width // 2, width), F32)
    return whole(
        exchange_kernel, [half, half], 1, 2, 4, (16 * 2 * 128 * 256 * 1024, 4),
    )(meta, near_blk, blk)


def base_kernel(meta_ref, orbs_ref, occ_ref, en_ref, amp_ref, own_ref,
                early_ref, keep_ref, recv_ref, out_ref):
    slots, rows, width = out_ref.shape
    holder, core = meta_ref[0], meta_ref[1]
    row0 = pl.multiple_of(core * rows, rows)

    @pl.loop(0, slots)
    def _(p):
        first, second = orbs_ref[0, p], orbs_ref[1, p]
        side = second // 2 - holder
        step = 1 - 2 * core
        index = 2 * (first % 2) + second % 2
        both = index + jnp.where(side == 0, 4, 0)
        cols = en_ref[pl.ds(p, 1), :]
        mine = jnp.where(core == 0, cols[:, :rows], cols[:, rows:])
        down = jnp.broadcast_to(mine, (rows, rows)).T
        down = jnp.concatenate([down] * (width // rows), axis=1)
        denom = down + cols - (occ_ref[first] + occ_ref[second])
        value = denom * amp_ref[p, pl.ds(row0, rows), :].astype(F32)
        value += own_ref[p]
        value += keep_ref[both] * jnp.where(side == -step, 0.0, 1.0)
        value += recv_ref[both] * jnp.where(side == step, 0.0, 1.0)
        out_ref[p] = value + early_ref[p].astype(F32)


def base(meta, orbs, occ, energy, amplitudes, own, early, keep, recv):
    return whole(
        base_kernel, jax.ShapeDtypeStruct(own.shape, F32), 3, 6, 4, (16 * 128 * 256 * 8, 8),
    )(meta, orbs, occ, energy, amplitudes, own, early, keep, recv)


def final_kernel(start, meta_ref, count_ref, orbs_ref, base_ref, far_ref, near_ref, *rest):
    out_hbm, buf, sem = rest[-3:]
    slots, rows, width = far_ref.shape
    row = lax.broadcasted_iota(jnp.int32, (rows, width), 0) + meta_ref[1] * rows
    col = lax.broadcasted_iota(jnp.int32, (rows, width), 1)
    most = jnp.maximum(row, col)

    def put(s):
        return pltpu.make_async_copy(buf.at[s], out_hbm.at[start + s], sem.at[s])

    @pl.loop(0, slots)
    def _(s):
        first, second = orbs_ref[0, start + s], orbs_ref[1, start + s]
        lacks = second // 2 - meta_ref[0] == 2 * meta_ref[1] - 1
        product = near_ref[2 * (first % 2) + second % 2].astype(F32)
        value = base_ref[start + s] + far_ref[s].astype(F32)
        value += product * jnp.where(lacks, 1.0, 0.0)
        buf[s] = jnp.where(most < count_ref[start + s], value, 0.0)
        put(s).start()

    @pl.loop(0, slots)
    def _(s):
        put(s).wait()


def final(start, meta, count, orbs, base_terms, far, near, earlier=None):
    slots, rows, width = far.shape
    smem = pl.BlockSpec(memory_space=SMEM)
    vmem = pl.BlockSpec(memory_space=VMEM)
    hbm = pl.BlockSpec(memory_space=pltpu.HBM)
    more = [] if earlier is None else [earlier]

    def kernel(*refs):
        final_kernel(start, *refs)

    return pl.pallas_call(
        kernel,
        out_shape=jax.ShapeDtypeStruct(base_terms.shape, F32),
        in_specs=[smem] * 3 + [vmem] * 3 + [hbm] * len(more),
        out_specs=hbm,
        scratch_shapes=[VMEM((slots, rows, width), F32), pltpu.SemaphoreType.DMA((slots,))],
        input_output_aliases={6: 0} if more else {},
        compiler_params=pltpu.CompilerParams(vmem_limit_bytes=4 * MIB),
        cost_estimate=pl.CostEstimate(
            flops=slots * 128 * 256 * 2, bytes_accessed=slots * MIB // 4, transcendentals=0),
    )(meta, count, orbs, base_terms, far, near, *more)


def local(blocks, pair_orbs, pno_count, amplitudes, margins, couple_target, couple_weight,
          pno_energy, occ_energy):
    holder = lax.axis_index("pairs").astype(jnp.int32)
    core = lax.axis_index("aux").astype(jnp.int32)
    holders = lax.axis_size("pairs")
    pairs, width = amplitudes.shape[0], amplitudes.shape[1]
    straight_in = toward(holders, False, True)
    straight_out = toward(holders, False, False)
    cross_out = toward(holders, True, False)
    swap = [(2 * h + c, 2 * h + 1 - c) for h in range(holders) for c in range(2)]

    orbs = pair_orbs.T
    near_blk = lax.ppermute(blocks, AXES, straight_in)
    near_orbs = lax.ppermute(orbs, AXES, straight_in)

    meta = jnp.stack([holder, core])
    rel = lax.dynamic_slice_in_dim(couple_target, holder * pairs, pairs, 0).T - holder * pairs
    weights = lax.dynamic_slice_in_dim(couple_weight, holder * pairs, pairs, 0).T
    rows = width // 2
    acc_far, msg_early = coupling(
        meta, rel, weights, amplitudes, margins, rows, rows)
    early = lax.ppermute(msg_early, AXES, straight_out)

    chunks = [pairs * 3 // 4, pairs - pairs * 3 // 4]
    msg_near, = message(
        near_kernel, [meta], [near_blk, blocks], [(4, rows)], width)
    near = lax.ppermute(msg_near, AXES, straight_out)
    msg_far = message(
        far_kernel, [meta, near_orbs], [near_blk, blocks, acc_far],
        [(n, rows) for n in chunks], width)
    far = lax.ppermute(msg_far[0], AXES, cross_out)
    last = lax.ppermute(msg_far[1], AXES, cross_out)

    keep, send = exchange(meta, near_blk, blocks)
    recv = lax.ppermute(send, AXES, swap)
    own, = coupling(meta, rel, weights, amplitudes, margins, rows, 0)
    base_terms = base(meta, orbs, occ_energy, pno_energy, amplitudes, own, early, keep, recv)
    out = final(0, meta, pno_count, orbs, base_terms, far, near)
    return final(chunks[0], meta, pno_count, orbs, base_terms, last, near, out)


def solution(mesh):
    placed = (
        P("pairs", "aux", None),
        P("pairs", None),
        P("pairs"),
        P("pairs", None, None),
        P("pairs", None, None, None),
        P(),
        P(),
        P("pairs", None),
        P(),
    )

    return jax.shard_map(
        local, mesh=mesh, in_specs=placed, out_specs=P("pairs", "aux", None), check_vma=False
    )
```

```python
import functools

import jax
import jax.numpy as jnp
from jax import lax
from jax.experimental import pallas as pl
from jax.experimental.pallas import tpu as pltpu
from jax.sharding import PartitionSpec as P

AXES = ("pairs", "aux")
BF16, F32 = jnp.bfloat16, jnp.float32
VMEM, SMEM = pltpu.VMEM, pltpu.SMEM
UNROLL = 4
MIB = 1 << 20


def toward(count, cross, flip):
    pairs = []
    for holder in range(count):
        for core in range(2):
            step = 1 if (core == 0) != flip else -1
            if 0 <= holder + step < count:
                dest = (1 - core) if cross else core
                pairs.append((2 * holder + core, 2 * (holder + step) + dest))
    return pairs


def nt_dot(a, b):
    return lax.dot_general(a, b, (((1,), (1,)), ((), ())), preferred_element_type=F32)


def tn_dot(a, b):
    return lax.dot_general(a, b, (((0,), (0,)), ((), ())), preferred_element_type=F32)


def coupling_kernel(early, meta_ref, rel_ref, w_ref, amp_hbm, mar_hbm, *rest):
    if early:
        far_ref, early_ref, mbuf, fbuf, items, msem, abuf, asem, acc_ref = rest
    else:
        (acc_ref, mbuf, fbuf, items, msem), abuf = rest, amp_hbm
    sources, couplings = mar_hbm.shape[0], mar_hbm.shape[1]
    slots, rows = acc_ref.shape[0], acc_ref.shape[1]
    core = meta_ref[1]
    shift = (1 - 2 * core) * slots if early else 0
    row0 = pl.multiple_of(core * rows, rows)
    far0 = pl.multiple_of(rows - core * rows, rows)

    def mar_copy(k):
        return pltpu.make_async_copy(
            mar_hbm.at[k // couplings, k % couplings], mbuf.at[k], msem.at[k])

    def amp_copy(q):
        return pltpu.make_async_copy(amp_hbm.at[q], abuf.at[q], asem.at[q])

    def scan(q, n):
        if early:
            amp_copy(q).start()
        for c in range(couplings):
            k = q * couplings + c
            slot = rel_ref[c, q] - shift
            mine = (slot >= 0) & (slot < slots)
            items[n] = k

            @pl.when(mine)
            def _():
                mar_copy(k).start()

            n = n + mine.astype(jnp.int32)
        return n

    n = lax.fori_loop(0, sources, scan, jnp.int32(0))
    for u in range(UNROLL):
        items[n + u] = items[0]

    @pl.loop(0, slots)
    def _(s):
        acc_ref[s] = jnp.zeros(acc_ref.shape[1:], F32)
        if early:
            far_ref[s] = jnp.zeros(acc_ref.shape[1:], F32)

    def wait_amp(q, x):
        amp_copy(q).wait()
        return x

    def body(g, waited):
        ks = [items[g * UNROLL + u] for u in range(UNROLL)]
        last = ks[0] // couplings
        for u in range(UNROLL):
            @pl.when(g * UNROLL + u < n)
            def _(u=u):
                mar_copy(ks[u]).wait()

            last = jnp.maximum(last, ks[u] // couplings)

        if early:
            lax.fori_loop(waited, last + 1, wait_amp, 0)
        for u in range(UNROLL):
            left = mbuf[ks[u], pl.ds(row0, rows), :]
            if early:
                left = jnp.concatenate([left, mbuf[ks[u], pl.ds(far0, rows), :]], axis=0)
            fbuf[u] = jnp.dot(
                left, abuf[ks[u] // couplings], preferred_element_type=F32).astype(BF16)
        for u in range(UNROLL):
            c, q = ks[u] % couplings, ks[u] // couplings
            weight = jnp.where(g * UNROLL + u < n, w_ref[c, q], 0.0)
            term = weight * nt_dot(fbuf[u], mbuf[ks[u]])
            acc_ref[rel_ref[c, q] - shift] += term[:rows]
            if early:
                far_ref[rel_ref[c, q] - shift] += term[rows:]
        return jnp.maximum(waited, last + 1)

    waited = lax.fori_loop(0, pl.cdiv(n, UNROLL), body, jnp.int32(0))
    if early:
        lax.fori_loop(waited, sources, wait_amp, 0)

        @pl.loop(0, slots)
        def _(s):
            early_ref[s] = acc_ref[s, :early].astype(BF16)


def coupling(meta, rel, weights, amplitudes, margins, rows, early):
    pairs, width = amplitudes.shape[0], amplitudes.shape[1]
    total = pairs * margins.shape[1]
    hbm = pl.BlockSpec(memory_space=pltpu.HBM)
    vmem = pl.BlockSpec(memory_space=VMEM)
    smem = pl.BlockSpec(memory_space=SMEM)
    out_shape = [jax.ShapeDtypeStruct((pairs, rows, width), F32)]
    scratch = [
        VMEM((total, width, width), BF16),
        VMEM((UNROLL, 2 * rows if early else rows, width), BF16),
        SMEM((total + UNROLL,), jnp.int32),
        pltpu.SemaphoreType.DMA((total,)),
    ]
    if early:
        amplitudes = pltpu.with_memory_space_constraint(amplitudes, pltpu.HBM)
        out_shape.append(jax.ShapeDtypeStruct((pairs, early, width), BF16))
        scratch += [VMEM((pairs, width, width), BF16), pltpu.SemaphoreType.DMA((pairs,)),
                    VMEM((pairs, rows, width), F32)]
    return pl.pallas_call(
        functools.partial(coupling_kernel, early),
        out_shape=out_shape,
        in_specs=[smem, smem, smem, hbm if early else vmem, hbm],
        out_specs=[vmem] * len(out_shape),
        scratch_shapes=scratch,
        compiler_params=pltpu.CompilerParams(vmem_limit_bytes=14 * MIB),
        cost_estimate=pl.CostEstimate(
            flops=2 * 22 * 2 * rows * 256 * 256, bytes_accessed=6 * MIB, transcendentals=0),
    )(meta, rel, weights, amplitudes, pltpu.with_memory_space_constraint(margins, pltpu.HBM))


def whole(kernel, out_shape, n_smem, n_vmem, limit, cost, **extra):
    vmem = pl.BlockSpec(memory_space=VMEM)
    return pl.pallas_call(
        kernel,
        out_shape=out_shape,
        in_specs=[pl.BlockSpec(memory_space=SMEM)] * n_smem + [vmem] * n_vmem,
        out_specs=jax.tree.map(lambda _: vmem, out_shape),
        compiler_params=pltpu.CompilerParams(vmem_limit_bytes=limit * MIB),
        cost_estimate=pl.CostEstimate(flops=cost[0], bytes_accessed=cost[1] * MIB, transcendentals=0),
        **extra,
    )


def products(far, near_blks, blk, meta_ref, prod):
    rows = prod.shape[1]
    for core in range(2):
        row0 = (1 - core if far else core) * rows

        @pl.when(meta_ref[1] == core)
        def _(near_blk=near_blks[core], row0=row0):
            for j in range(2):
                for i in range(2):
                    prod[2 * j + i] = tn_dot(near_blk[j, :, row0:row0 + rows], blk[i])

    prod[4] = jnp.zeros(prod.shape[1:], F32)


def pick(meta_ref, orbs_ref, s):
    second = orbs_ref[1, s] - 2 * meta_ref[0]
    mine = (second >= 0) & (second < 2)
    return jnp.where(mine, 2 * (orbs_ref[0, s] % 2) + second, 4)


def near_kernel(meta_ref, next_blk, prev_blk, blk, out, prod):
    products(False, (next_blk, prev_blk), blk, meta_ref, prod)
    for k in range(4):
        out[k] = prod[k].astype(BF16)


def far_kernel(meta_ref, orbs_ref, next_blk, prev_blk, blk, acc_ref, *rest):
    out_refs, prod = rest[:-1], rest[-1]
    products(True, (next_blk, prev_blk), blk, meta_ref, prod)
    start = 0
    for out in out_refs:
        @pl.loop(0, out.shape[0])
        def _(s, out=out, start=start):
            out[s] = (acc_ref[start + s]
                      + prod[pick(meta_ref, orbs_ref, start + s)]).astype(BF16)

        start += out.shape[0]


def message(kernel, smem, vmem, outs, width):
    return whole(
        kernel,
        [jax.ShapeDtypeStruct((*n, width), BF16) for n in outs],
        len(smem), len(vmem), 4, (4 * 2 * 128 * 256 * 1024, 4),
        scratch_shapes=[VMEM((5, width // 2, width), F32)],
    )(*smem, *vmem)


def exchange_kernel(meta_ref, next_blk, prev_blk, blk, keep_ref, send_ref):
    rows = keep_ref.shape[1]
    for core, near_blk in enumerate((next_blk, prev_blk)):
        @pl.when(meta_ref[1] == core)
        def _(core=core, near_blk=near_blk):
            for out, side in ((keep_ref, core), (send_ref, 1 - core)):
                for i in range(2):
                    left = blk[i, :, side * rows:(side + 1) * rows]
                    for j in range(2):
                        out[2 * i + j] = tn_dot(left, near_blk[j])
                        out[4 + 2 * i + j] = tn_dot(left, blk[j])


def exchange(meta, next_blk, prev_blk, blk):
    width = blk.shape[2]
    half = jax.ShapeDtypeStruct((8, width // 2, width), F32)
    return whole(
        exchange_kernel, [half, half], 1, 3, 4, (16 * 2 * 128 * 256 * 1024, 4),
    )(meta, next_blk, prev_blk, blk)


def base_kernel(meta_ref, orbs_ref, occ_ref, en_ref, amp_ref, own_ref,
                early_ref, keep_ref, recv_ref, out_ref):
    slots, rows, width = out_ref.shape
    holder, core = meta_ref[0], meta_ref[1]
    row0 = pl.multiple_of(core * rows, rows)

    @pl.loop(0, slots)
    def _(p):
        first, second = orbs_ref[0, p], orbs_ref[1, p]
        side = second // 2 - holder
        step = 1 - 2 * core
        index = 2 * (first % 2) + second % 2
        both = index + jnp.where(side == 0, 4, 0)
        cols = en_ref[pl.ds(p, 1), :]
        mine = jnp.where(core == 0, cols[:, :rows], cols[:, rows:])
        down = jnp.broadcast_to(mine, (rows, rows)).T
        down = jnp.concatenate([down] * (width // rows), axis=1)
        denom = down + cols - (occ_ref[first] + occ_ref[second])
        value = denom * amp_ref[p, pl.ds(row0, rows), :].astype(F32)
        value += own_ref[p]
        value += keep_ref[both] * jnp.where(side == -step, 0.0, 1.0)
        value += recv_ref[both] * jnp.where(side == step, 0.0, 1.0)
        out_ref[p] = value + early_ref[p].astype(F32)


def base(meta, orbs, occ, energy, amplitudes, own, early, keep, recv):
    return whole(
        base_kernel, jax.ShapeDtypeStruct(own.shape, F32), 3, 6, 4, (16 * 128 * 256 * 8, 8),
    )(meta, orbs, occ, energy, amplitudes, own, early, keep, recv)


def final_kernel(start, meta_ref, count_ref, orbs_ref, base_ref, far_ref, near_ref, *rest):
    out_hbm, buf, sem = rest[-3:]
    slots, rows, width = far_ref.shape
    row = lax.broadcasted_iota(jnp.int32, (rows, width), 0) + meta_ref[1] * rows
    col = lax.broadcasted_iota(jnp.int32, (rows, width), 1)
    most = jnp.maximum(row, col)

    def put(s):
        return pltpu.make_async_copy(buf.at[s], out_hbm.at[start + s], sem.at[s])

    @pl.loop(0, slots)
    def _(s):
        first, second = orbs_ref[0, start + s], orbs_ref[1, start + s]
        lacks = second // 2 - meta_ref[0] == 2 * meta_ref[1] - 1
        product = near_ref[2 * (first % 2) + second % 2].astype(F32)
        value = base_ref[start + s] + far_ref[s].astype(F32)
        value += product * jnp.where(lacks, 1.0, 0.0)
        buf[s] = jnp.where(most < count_ref[start + s], value, 0.0)
        put(s).start()

    @pl.loop(0, slots)
    def _(s):
        put(s).wait()


def final(start, meta, count, orbs, base_terms, far, near, earlier=None):
    slots, rows, width = far.shape
    smem = pl.BlockSpec(memory_space=SMEM)
    vmem = pl.BlockSpec(memory_space=VMEM)
    hbm = pl.BlockSpec(memory_space=pltpu.HBM)
    more = [] if earlier is None else [earlier]

    def kernel(*refs):
        final_kernel(start, *refs)

    return pl.pallas_call(
        kernel,
        out_shape=jax.ShapeDtypeStruct(base_terms.shape, F32),
        in_specs=[smem] * 3 + [vmem] * 3 + [hbm] * len(more),
        out_specs=hbm,
        scratch_shapes=[VMEM((slots, rows, width), F32), pltpu.SemaphoreType.DMA((slots,))],
        input_output_aliases={6: 0} if more else {},
        compiler_params=pltpu.CompilerParams(vmem_limit_bytes=4 * MIB),
        cost_estimate=pl.CostEstimate(
            flops=slots * 128 * 256 * 2, bytes_accessed=slots * MIB // 4, transcendentals=0),
    )(meta, count, orbs, base_terms, far, near, *more)


def local(blocks, pair_orbs, pno_count, amplitudes, margins, couple_target, couple_weight,
          pno_energy, occ_energy):
    holder = lax.axis_index("pairs").astype(jnp.int32)
    core = lax.axis_index("aux").astype(jnp.int32)
    holders = lax.axis_size("pairs")
    pairs, width = amplitudes.shape[0], amplitudes.shape[1]
    straight_in = toward(holders, False, True)
    straight_out = toward(holders, False, False)
    cross_out = toward(holders, True, False)
    swap = [(2 * h + c, 2 * h + 1 - c) for h in range(holders) for c in range(2)]

    orbs = pair_orbs.T
    prev_blk = lax.ppermute(blocks, AXES, [(s, t) for s, t in straight_in if s % 2 == 1])
    next_blk = lax.ppermute(blocks, AXES, [(s, t) for s, t in straight_in if s % 2 == 0])
    near_orbs = lax.ppermute(orbs, AXES, straight_in)

    meta = jnp.stack([holder, core])
    rel = lax.dynamic_slice_in_dim(couple_target, holder * pairs, pairs, 0).T - holder * pairs
    weights = lax.dynamic_slice_in_dim(couple_weight, holder * pairs, pairs, 0).T
    rows = width // 2
    acc_far, msg_early = coupling(
        meta, rel, weights, amplitudes, margins, rows, rows)
    early = lax.ppermute(msg_early, AXES, straight_out)

    chunks = [pairs * 3 // 4, pairs - pairs * 3 // 4]
    msg_near, = message(
        near_kernel, [meta], [next_blk, prev_blk, blocks], [(4, rows)], width)
    near = lax.ppermute(msg_near, AXES, straight_out)
    msg_far = message(
        far_kernel, [meta, near_orbs], [next_blk, prev_blk, blocks, acc_far],
        [(n, rows) for n in chunks], width)
    far = lax.ppermute(msg_far[0], AXES, cross_out)
    last = lax.ppermute(msg_far[1], AXES, cross_out)

    keep, send = exchange(meta, next_blk, prev_blk, blocks)
    recv = lax.ppermute(send, AXES, swap)
    own, = coupling(meta, rel, weights, amplitudes, margins, rows, 0)
    base_terms = base(meta, orbs, occ_energy, pno_energy, amplitudes, own, early, keep, recv)
    out = final(0, meta, pno_count, orbs, base_terms, far, near)
    return final(chunks[0], meta, pno_count, orbs, base_terms, last, near, out)


def solution(mesh):
    placed = (
        P("pairs", "aux", None),
        P("pairs", None),
        P("pairs"),
        P("pairs", None, None),
        P("pairs", None, None, None),
        P(),
        P(),
        P("pairs", None),
        P(),
    )

    return jax.shard_map(
        local, mesh=mesh, in_specs=placed, out_specs=P("pairs", "aux", None), check_vma=False
    )
```

```python
import functools

import jax
import jax.numpy as jnp
from jax import lax
from jax.experimental import pallas as pl
from jax.experimental.pallas import tpu as pltpu
from jax.sharding import PartitionSpec as P

AXES = ("pairs", "aux")
BF16, F32 = jnp.bfloat16, jnp.float32
VMEM, SMEM = pltpu.VMEM, pltpu.SMEM
UNROLL = 4
MIB = 1 << 20


def toward(count, cross, flip):
    pairs = []
    for holder in range(count):
        for core in range(2):
            step = 1 if (core == 0) != flip else -1
            if 0 <= holder + step < count:
                dest = (1 - core) if cross else core
                pairs.append((2 * holder + core, 2 * (holder + step) + dest))
    return pairs


def nt_dot(a, b):
    return lax.dot_general(a, b, (((1,), (1,)), ((), ())), preferred_element_type=F32)


def tn_dot(a, b):
    return lax.dot_general(a, b, (((0,), (0,)), ((), ())), preferred_element_type=F32)


def coupling_kernel(early, meta_ref, rel_ref, w_ref, amp_hbm, mar_hbm, *rest):
    if early:
        far_ref, early_ref, mbuf, fbuf, items, msem, abuf, asem, acc_ref = rest
    else:
        (acc_ref, mbuf, fbuf, items, msem), abuf = rest, amp_hbm
    sources, couplings = mar_hbm.shape[0], mar_hbm.shape[1]
    slots, rows = acc_ref.shape[0], acc_ref.shape[1]
    core = meta_ref[1]
    shift = (2 * core - 1) * slots if early else 0
    row0 = pl.multiple_of(core * rows, rows)
    far0 = pl.multiple_of(rows - core * rows, rows)

    def mar_copy(k):
        return pltpu.make_async_copy(
            mar_hbm.at[k // couplings, k % couplings], mbuf.at[k], msem.at[k])

    def amp_copy(q):
        return pltpu.make_async_copy(amp_hbm.at[q], abuf.at[q], asem.at[q])

    def scan(q, n):
        if early:
            amp_copy(q).start()
        for c in range(couplings):
            k = q * couplings + c
            slot = rel_ref[c, q] - shift
            mine = (slot >= 0) & (slot < slots)
            items[n] = k

            @pl.when(mine)
            def _():
                mar_copy(k).start()

            n = n + mine.astype(jnp.int32)
        return n

    n = lax.fori_loop(0, sources, scan, jnp.int32(0))
    for u in range(UNROLL):
        items[n + u] = items[0]

    @pl.loop(0, slots)
    def _(s):
        acc_ref[s] = jnp.zeros(acc_ref.shape[1:], F32)
        if early:
            far_ref[s] = jnp.zeros(acc_ref.shape[1:], F32)

    def wait_amp(q, x):
        amp_copy(q).wait()
        return x

    def body(g, waited):
        ks = [items[g * UNROLL + u] for u in range(UNROLL)]
        last = ks[0] // couplings
        for u in range(UNROLL):
            @pl.when(g * UNROLL + u < n)
            def _(u=u):
                mar_copy(ks[u]).wait()

            last = jnp.maximum(last, ks[u] // couplings)

        if early:
            lax.fori_loop(waited, last + 1, wait_amp, 0)
        for u in range(UNROLL):
            left = mbuf[ks[u], pl.ds(row0, rows), :]
            if early:
                left = jnp.concatenate([left, mbuf[ks[u], pl.ds(far0, rows), :]], axis=0)
            fbuf[u] = jnp.dot(
                left, abuf[ks[u] // couplings], preferred_element_type=F32).astype(BF16)
        for u in range(UNROLL):
            c, q = ks[u] % couplings, ks[u] // couplings
            weight = jnp.where(g * UNROLL + u < n, w_ref[c, q], 0.0)
            term = weight * nt_dot(fbuf[u], mbuf[ks[u]])
            acc_ref[rel_ref[c, q] - shift] += term[:rows]
            if early:
                far_ref[rel_ref[c, q] - shift] += term[rows:]
        return jnp.maximum(waited, last + 1)

    waited = lax.fori_loop(0, pl.cdiv(n, UNROLL), body, jnp.int32(0))
    if early:
        lax.fori_loop(waited, sources, wait_amp, 0)

        @pl.loop(0, slots)
        def _(s):
            early_ref[s] = acc_ref[s, :early].astype(BF16)


def coupling(meta, rel, weights, amplitudes, margins, rows, early):
    pairs, width = amplitudes.shape[0], amplitudes.shape[1]
    total = pairs * margins.shape[1]
    hbm = pl.BlockSpec(memory_space=pltpu.HBM)
    vmem = pl.BlockSpec(memory_space=VMEM)
    smem = pl.BlockSpec(memory_space=SMEM)
    out_shape = [jax.ShapeDtypeStruct((pairs, rows, width), F32)]
    scratch = [
        VMEM((total, width, width), BF16),
        VMEM((UNROLL, 2 * rows if early else rows, width), BF16),
        SMEM((total + UNROLL,), jnp.int32),
        pltpu.SemaphoreType.DMA((total,)),
    ]
    if early:
        amplitudes = pltpu.with_memory_space_constraint(amplitudes, pltpu.HBM)
        out_shape.append(jax.ShapeDtypeStruct((pairs, early, width), BF16))
        scratch += [VMEM((pairs, width, width), BF16), pltpu.SemaphoreType.DMA((pairs,)),
                    VMEM((pairs, rows, width), F32)]
    return pl.pallas_call(
        functools.partial(coupling_kernel, early),
        out_shape=out_shape,
        in_specs=[smem, smem, smem, hbm if early else vmem, hbm],
        out_specs=[vmem] * len(out_shape),
        scratch_shapes=scratch,
        compiler_params=pltpu.CompilerParams(vmem_limit_bytes=14 * MIB),
        cost_estimate=pl.CostEstimate(
            flops=2 * 22 * 2 * rows * 256 * 256, bytes_accessed=6 * MIB, transcendentals=0),
    )(meta, rel, weights, amplitudes, pltpu.with_memory_space_constraint(margins, pltpu.HBM))


def whole(kernel, out_shape, n_smem, n_vmem, limit, cost, **extra):
    vmem = pl.BlockSpec(memory_space=VMEM)
    return pl.pallas_call(
        kernel,
        out_shape=out_shape,
        in_specs=[pl.BlockSpec(memory_space=SMEM)] * n_smem + [vmem] * n_vmem,
        out_specs=jax.tree.map(lambda _: vmem, out_shape),
        compiler_params=pltpu.CompilerParams(vmem_limit_bytes=limit * MIB),
        cost_estimate=pl.CostEstimate(flops=cost[0], bytes_accessed=cost[1] * MIB, transcendentals=0),
        **extra,
    )


def products(far, near_blk, blk, meta_ref, prod):
    rows = prod.shape[1]
    core = meta_ref[1]
    row0 = pl.multiple_of((1 - core if far else core) * rows, rows)
    for j in range(2):
        for i in range(2):
            prod[2 * j + i] = tn_dot(near_blk[j, :, pl.ds(row0, rows)], blk[i])
    prod[4] = jnp.zeros(prod.shape[1:], F32)


def pick(meta_ref, orbs_ref, s):
    second = orbs_ref[1, s] - 2 * meta_ref[0]
    mine = (second >= 0) & (second < 2)
    return jnp.where(mine, 2 * (orbs_ref[0, s] % 2) + second, 4)


def near_kernel(meta_ref, near_blk, blk, out, prod):
    products(False, near_blk, blk, meta_ref, prod)
    for k in range(4):
        out[k] = prod[k].astype(BF16)


def far_kernel(meta_ref, orbs_ref, near_blk, blk, acc_ref, *rest):
    out_refs, prod = rest[:-1], rest[-1]
    products(True, near_blk, blk, meta_ref, prod)
    start = 0
    for out in out_refs:
        @pl.loop(0, out.shape[0])
        def _(s, out=out, start=start):
            out[s] = (acc_ref[start + s]
                      + prod[pick(meta_ref, orbs_ref, start + s)]).astype(BF16)

        start += out.shape[0]


def message(kernel, smem, vmem, outs, width):
    return whole(
        kernel,
        [jax.ShapeDtypeStruct((*n, width), BF16) for n in outs],
        len(smem), len(vmem), 4, (4 * 2 * 128 * 256 * 1024, 4),
        scratch_shapes=[VMEM((5, width // 2, width), F32)],
    )(*smem, *vmem)


def exchange_kernel(meta_ref, near_blk, swapped, blk, keep_ref, send_ref):
    rows = keep_ref.shape[1]
    for out, side in ((keep_ref, meta_ref[1]), (send_ref, 1 - meta_ref[1])):
        row0 = pl.multiple_of(side * rows, rows)
        for i in range(2):
            other = swapped[i, :, pl.ds(row0, rows)]
            left = blk[i, :, pl.ds(row0, rows)]
            for j in range(2):
                out[2 * i + j] = tn_dot(other, near_blk[j])
                out[4 + 2 * i + j] = tn_dot(left, blk[j])


def exchange(meta, near_blk, swapped, blk):
    width = blk.shape[2]
    half = jax.ShapeDtypeStruct((8, width // 2, width), F32)
    return whole(
        exchange_kernel, [half, half], 1, 3, 4, (16 * 2 * 128 * 256 * 1024, 4),
    )(meta, near_blk, swapped, blk)


def base_kernel(meta_ref, orbs_ref, occ_ref, en_ref, amp_ref, own_ref,
                early_ref, near_ref, keep_ref, recv_ref, out_ref):
    slots, rows, width = out_ref.shape
    holder, core = meta_ref[0], meta_ref[1]
    row0 = pl.multiple_of(core * rows, rows)

    @pl.loop(0, slots)
    def _(p):
        first, second = orbs_ref[0, p], orbs_ref[1, p]
        side = second // 2 - holder
        step = 2 * core - 1
        index = 2 * (first % 2) + second % 2
        both = index + jnp.where(side == 0, 4, 0)
        cols = en_ref[pl.ds(p, 1), :]
        mine = jnp.where(core == 0, cols[:, :rows], cols[:, rows:])
        down = jnp.broadcast_to(mine, (rows, rows)).T
        down = jnp.concatenate([down] * (width // rows), axis=1)
        denom = down + cols - (occ_ref[first] + occ_ref[second])
        value = denom * amp_ref[p, pl.ds(row0, rows), :].astype(F32)
        value += own_ref[p]
        value += keep_ref[both] * jnp.where(side == -step, 0.0, 1.0)
        value += recv_ref[both] * jnp.where(side == step, 0.0, 1.0)
        value += near_ref[index].astype(F32) * jnp.where(side == -step, 1.0, 0.0)
        out_ref[p] = value + early_ref[p].astype(F32)


def base(meta, orbs, occ, energy, amplitudes, own, early, near, keep, recv):
    return whole(
        base_kernel, jax.ShapeDtypeStruct(own.shape, F32), 3, 7, 4, (16 * 128 * 256 * 8, 8),
    )(meta, orbs, occ, energy, amplitudes, own, early, near, keep, recv)


def final_kernel(start, meta_ref, count_ref, base_ref, far_ref, *rest):
    out_hbm, buf, sem = rest[-3:]
    slots, rows, width = far_ref.shape
    row = lax.broadcasted_iota(jnp.int32, (rows, width), 0) + meta_ref[1] * rows
    col = lax.broadcasted_iota(jnp.int32, (rows, width), 1)
    most = jnp.maximum(row, col)

    def put(s):
        return pltpu.make_async_copy(buf.at[s], out_hbm.at[start + s], sem.at[s])

    @pl.loop(0, slots)
    def _(s):
        value = base_ref[start + s] + far_ref[s].astype(F32)
        buf[s] = jnp.where(most < count_ref[start + s], value, 0.0)
        put(s).start()

    @pl.loop(0, slots)
    def _(s):
        put(s).wait()


def final(start, meta, count, base_terms, far, earlier=None):
    slots, rows, width = far.shape
    smem = pl.BlockSpec(memory_space=SMEM)
    vmem = pl.BlockSpec(memory_space=VMEM)
    hbm = pl.BlockSpec(memory_space=pltpu.HBM)
    more = [] if earlier is None else [earlier]

    def kernel(*refs):
        final_kernel(start, *refs)

    return pl.pallas_call(
        kernel,
        out_shape=jax.ShapeDtypeStruct(base_terms.shape, F32),
        in_specs=[smem, smem, vmem, vmem] + [hbm] * len(more),
        out_specs=hbm,
        scratch_shapes=[VMEM((slots, rows, width), F32), pltpu.SemaphoreType.DMA((slots,))],
        input_output_aliases={4: 0} if more else {},
        compiler_params=pltpu.CompilerParams(vmem_limit_bytes=4 * MIB),
        cost_estimate=pl.CostEstimate(
            flops=slots * 128 * 256 * 2, bytes_accessed=slots * MIB // 4, transcendentals=0),
    )(meta, count, base_terms, far, *more)


def local(blocks, pair_orbs, pno_count, amplitudes, margins, couple_target, couple_weight,
          pno_energy, occ_energy):
    holder = lax.axis_index("pairs").astype(jnp.int32)
    core = lax.axis_index("aux").astype(jnp.int32)
    holders = lax.axis_size("pairs")
    pairs, width = amplitudes.shape[0], amplitudes.shape[1]
    straight_out = toward(holders, False, True)
    cross_out = toward(holders, True, True)
    swap = [(2 * h + c, 2 * h + 1 - c) for h in range(holders) for c in range(2)]

    orbs = pair_orbs.T
    near_blk = lax.ppermute(blocks, AXES, cross_out)
    near_orbs = lax.ppermute(orbs, AXES, cross_out)

    meta = jnp.stack([holder, core])
    rel = lax.dynamic_slice_in_dim(couple_target, holder * pairs, pairs, 0).T - holder * pairs
    weights = lax.dynamic_slice_in_dim(couple_weight, holder * pairs, pairs, 0).T
    rows = width // 2
    acc_far, msg_early = coupling(
        meta, rel, weights, amplitudes, margins, rows, rows)
    early = lax.ppermute(msg_early, AXES, straight_out)
    swapped = lax.ppermute(blocks, AXES, swap)

    chunks = [pairs * 3 // 4, pairs - pairs * 3 // 4]
    msg_near, = message(
        near_kernel, [meta], [near_blk, swapped], [(4, rows)], width)
    near = lax.ppermute(msg_near, AXES, straight_out)
    msg_far = message(
        far_kernel, [meta, near_orbs], [near_blk, swapped, acc_far],
        [(n, rows) for n in chunks], width)
    far = lax.ppermute(msg_far[0], AXES, cross_out)
    last = lax.ppermute(msg_far[1], AXES, cross_out)

    keep, send = exchange(meta, near_blk, swapped, blocks)
    recv = lax.ppermute(send, AXES, swap)
    own, = coupling(meta, rel, weights, amplitudes, margins, rows, 0)
    base_terms = base(meta, orbs, occ_energy, pno_energy, amplitudes, own, early, near,
                      keep, recv)
    out = final(0, meta, pno_count, base_terms, far)
    return final(chunks[0], meta, pno_count, base_terms, last, out)


def solution(mesh):
    placed = (
        P("pairs", "aux", None),
        P("pairs", None),
        P("pairs"),
        P("pairs", None, None),
        P("pairs", None, None, None),
        P(),
        P(),
        P("pairs", None),
        P(),
    )

    return jax.shard_map(
        local, mesh=mesh, in_specs=placed, out_specs=P("pairs", "aux", None), check_vma=False
    )
```
